128 devices in a mesh: expert: 32 (over z, x, core), dp: 4 (over y).
Axes of the slice: x: 4, y: 4, z: 4, core: 2. Of those that a mesh axis runs over, the one named last changes fastest.
Arguments:
- tokens: bfloat16 [16384, 2048], P(('expert', 'dp')), may hold values from -6 to 6
- out_grad: bfloat16 [16384, 2048], P(('expert', 'dp')), may hold values from -6 to 6
- route_weights: bfloat16 [16384, 8], P(('expert', 'dp')), may hold values from 0.05 to 2.5, as said below
- expert_ids: int32 [16384, 8], P(('expert', 'dp')), may hold values from 0 to 63, all different within a row; in each aligned block of 128 rows (0 to 127, 128 to 255, ...) at most 24 rows name the same one
- gate_weight: bfloat16 [64, 2048, 384], P('expert'), may hold values from -0.125 to 0.125
- up_weight: bfloat16 [64, 2048, 384], P('expert'), may hold values from -0.125 to 0.125
- down_weight: bfloat16 [64, 384, 2048], P('expert'), may hold values from -0.3125 to 0.3125
Outputs:
- grad_input: bfloat16 [16384, 2048], P(('expert', 'dp'))
- grad_gate: bfloat16 [64, 2048, 384], P('expert', 'dp')
- grad_up: bfloat16 [64, 2048, 384], P('expert', 'dp')
- grad_down: bfloat16 [64, 384, 2048], P('expert', 'dp')
- expert_load: float32 [64], replicated
The draws below stay inside these ranges and needn't reach their ends.
Inputs may be any that keep to these rules, and one draw needn't show every extreme that they name: `expert_ids`: each row names 8 different experts. Within each aligned block of 128 rows (the rows of one device) no expert is named by more than 24 rows, a bound that some block reaches. `route_weights`: positive router weights.
All inputs are finite; a program needn't handle non-finite values.
Results may differ from the reference program's by a relative error of at most 0.009.
Values may be sent and summed in bfloat16 or wider, within the bound.
A program may use at most 192 MiB of HBM per device.

```python
import math
import jax
import jax.numpy as jnp
import numpy as np
from jax import lax

D = 2048
F = 384
TOP = 8
TOK_DEV = 128
EXPERTS = 64
CAP = 24
TOKENS = 16384
N_EXPERT = 32
N_DP = 4


def draw_route_weights(key, part):
    row_share = jnp.arange(TOKENS, dtype=jnp.float32)[:, None] / (TOKENS - 1)
    lowest = jnp.log(0.05)
    highest = jnp.log(0.5)
    base = jnp.exp(jax.random.uniform(key, (TOKENS, TOP), jnp.float32, lowest, highest))
    ramp = 1.0 + 2.0 * row_share
    return (base * ramp).astype(jnp.bfloat16)


def shard_levels(key, shape, shards, least, top_value):
    factor_of = 1.0
    for position, shards_of in shards:
        steps = jax.random.uniform(jax.random.fold_in(jax.random.fold_in(key, 6), position), (shards_of,), jnp.float32, least / len(shards), top_value / len(shards))
        factor_of = factor_of * jnp.repeat(jnp.exp(steps), shape[position] // shards_of).reshape((-1,) + (1,) * (len(shape) - 1 - position))
    return factor_of


def assign_block(key, own, number, rows, number_of, top, reach, skew):
    ranking = jax.random.permutation(key, number_of)
    heavy_load, common = load_shares(number_of, rows * top, reach, skew, True), load_shares(number_of, rows * top, reach, skew, False)
    places = jnp.arange(number_of)

    def named(sizes, offset_by):
        used = int((sizes > 0).sum())
        fixed = max(1, used // 4)
        moved = fixed + (places - fixed + offset_by * (used - fixed)) % max(1, number_of - fixed)
        return jnp.zeros((number_of,), jnp.int32).at[ranking[jnp.where(places < fixed, places, moved)]].set(jnp.asarray(sizes, jnp.int32))

    sizes = jnp.where(number % 4 == 0, named(heavy_load, number // 4), named(common, number - number // 4 - 1))
    mixed = jax.random.permutation(jax.random.fold_in(own, 3), number_of)
    source_of, sink = mixed[0:number_of // 2 * 2:2], mixed[1:number_of // 2 * 2:2]
    room = jnp.minimum(sizes[source_of] - 1, reach - sizes[sink]) // 2
    room = jnp.where((source_of == ranking[0]) | (sink == ranking[0]) | (sizes[sink] == 0), 0, jnp.maximum(room, 0))
    moved = jax.random.randint(jax.random.fold_in(own, 4), (number_of // 2,), 0, 1 << 20) % (room + 1)
    sizes = sizes.at[source_of].add(-moved).at[sink].add(moved)
    labels = jnp.searchsorted(jnp.cumsum(sizes), jnp.arange(rows * top), side="right").astype(jnp.int32)
    listing = labels.reshape(top, rows).T
    listing = listing[jax.random.permutation(jax.random.fold_in(own, 1), rows)]
    offset_by = jax.random.randint(jax.random.fold_in(own, 2), (rows, 1), 0, top)
    return jnp.take_along_axis(listing, (jnp.arange(top)[None, :] + offset_by) % top, axis=1)


def load_shares(count, total, most, slope, full):
    weights = [(1 << 20) // math.isqrt(grade ** slope) + 1 for grade in range(1, count + 1)]
    largest = most if full else min(most, max(-(-total // count), total * weights[0] // sum(weights)))
    least = 1 if total - largest >= count - 1 else 0
    holding, rest = [largest] + [least] * (count - 1), total - largest - least * (count - 1)
    while rest > 0:
        free = [i for i in range(1, count) if holding[i] < largest] or [i for i in range(1, count) if holding[i] < most]
        mass, left = sum([weights[i] for i in free]), rest
        for i in free:
            addition = min(most - holding[i], max(1, left * weights[i] // mass), rest)
            holding[i] = holding[i] + addition
            rest = rest - addition
    return np.array(holding)


def normal_values(rng, shape, scale, bound, cuts=(), kind=jnp.bfloat16):
    loudness = shard_levels(rng, shape, cuts, -0.22, 0.18) if cuts else 1.0
    array = jax.random.normal(rng, shape, jnp.float32) * scale * loudness
    return jnp.minimum(jnp.maximum(array, -bound), bound).astype(kind)


def setup_inputs(seed: int = 0) -> dict:
    streams_of = jax.random.split(jax.random.key(seed), 8)
    tokens = normal_values(streams_of[0], (TOKENS, D), 1.0, 6.0, ((0, 128),))
    out_grad = normal_values(streams_of[1], (TOKENS, D), 1.0, 6.0, ((0, 128),))
    route_weights = draw_route_weights(jax.random.fold_in(streams_of[7], 71), 0)
    expert_ids_keys = jax.random.split(jax.random.fold_in(streams_of[3], 1), TOKENS // TOK_DEV)
    expert_ids_turns = jax.random.permutation(jax.random.fold_in(streams_of[3], 3), TOKENS // TOK_DEV)
    expert_ids = jax.vmap(lambda own, number: assign_block(jax.random.fold_in(streams_of[3], 2), own, number, TOK_DEV, EXPERTS, TOP, CAP, 2))(expert_ids_keys, expert_ids_turns).reshape((TOKENS, TOP))
    gate_weight = normal_values(streams_of[4], (EXPERTS, D, F), D ** -0.5, 0.125, ((0, 32),))
    up_weight = normal_values(streams_of[5], (EXPERTS, D, F), D ** -0.5, 0.125, ((0, 32),))
    down_weight = normal_values(streams_of[6], (EXPERTS, F, D), F ** -0.5, 0.3125, ((0, 32),))
    return dict(tokens=tokens, out_grad=out_grad, route_weights=route_weights, expert_ids=expert_ids, gate_weight=gate_weight, up_weight=up_weight, down_weight=down_weight)


def swiglu_grads(token_rows, grad_rows, route_rows, gate_matrix, up_matrix, down_matrix):
    contract_last = (((1,), (1,)), ((), ()))
    contract_first = (((0,), (0,)), ((), ()))
    gate_linear = jnp.dot(token_rows, gate_matrix, preferred_element_type=jnp.float32)
    up_linear = jnp.dot(token_rows, up_matrix, preferred_element_type=jnp.float32)
    logistic = jax.nn.sigmoid(gate_linear)
    activated = gate_linear * logistic
    hidden = (activated * up_linear).astype(jnp.bfloat16)
    scaled = (route_rows.astype(jnp.float32)[:, None] * grad_rows.astype(jnp.float32)).astype(jnp.bfloat16)
    delta_hidden = lax.dot_general(scaled, down_matrix, contract_last, preferred_element_type=jnp.float32)
    delta_gate = (delta_hidden * up_linear * logistic * (1.0 + gate_linear * (1.0 - logistic))).astype(jnp.bfloat16)
    delta_up = (delta_hidden * activated).astype(jnp.bfloat16)
    pair_grad = lax.dot_general(delta_gate, gate_matrix, contract_last, preferred_element_type=jnp.float32)
    pair_grad = pair_grad + lax.dot_general(delta_up, up_matrix, contract_last, preferred_element_type=jnp.float32)
    gate_part = lax.dot_general(token_rows, delta_gate, contract_first, preferred_element_type=jnp.float32)
    up_part = lax.dot_general(token_rows, delta_up, contract_first, preferred_element_type=jnp.float32)
    down_part = lax.dot_general(hidden, scaled, contract_first, preferred_element_type=jnp.float32)
    return pair_grad, gate_part, up_part, down_part


def reference(tokens, out_grad, route_weights, expert_ids, gate_weight, up_weight, down_weight):
    num_experts = gate_weight.shape[0]
    blocks = N_EXPERT * N_DP
    token_total = tokens.shape[0]
    block_ids = expert_ids.reshape(blocks, TOK_DEV, TOP).astype(jnp.int32)
    expert_iota = jnp.arange(num_experts, dtype=jnp.int32)
    per_token = jnp.sum((block_ids[..., None] == expert_iota).astype(jnp.int32), axis=2)
    route_blocks = route_weights.reshape(blocks, TOK_DEV, TOP).astype(jnp.float32)
    expert_weight = jnp.sum(jnp.where(block_ids[..., None] == expert_iota, route_blocks[..., None], jnp.zeros((), jnp.float32)), axis=(0, 1, 2))
    expert_load = expert_weight * (num_experts / (token_total * TOP))
    earlier = jnp.cumsum(per_token, axis=1) - per_token
    rank_in_block = jnp.take_along_axis(earlier, block_ids, axis=2).astype(jnp.int32)
    block_iota = jnp.arange(blocks, dtype=jnp.int32)[:, None, None]
    token_iota = block_iota * TOK_DEV + jnp.arange(TOK_DEV, dtype=jnp.int32)[None, :, None] + jnp.zeros_like(block_ids)
    slot_place = ((block_ids * blocks + block_iota) * CAP + rank_in_block).reshape(-1).astype(jnp.int32)
    slot_table = jnp.full((num_experts * blocks * CAP,), token_total, jnp.int32)
    slot_table = slot_table.at[slot_place].set(token_iota.reshape(-1).astype(jnp.int32))
    weight_table = jnp.zeros((num_experts * blocks * CAP,), jnp.float32)
    weight_table = weight_table.at[slot_place].set(route_weights.reshape(-1).astype(jnp.float32))
    slot_table = slot_table.reshape(num_experts, N_EXPERT, N_DP, CAP).transpose(0, 2, 1, 3).reshape(num_experts, N_DP, N_EXPERT * CAP)
    weight_table = weight_table.reshape(num_experts, N_EXPERT, N_DP, CAP).transpose(0, 2, 1, 3).reshape(num_experts, N_DP, N_EXPERT * CAP)
    padded_tokens = jnp.concatenate([tokens, jnp.zeros((1, D), tokens.dtype)], axis=0)
    padded_grads = jnp.concatenate([out_grad, jnp.zeros((1, D), out_grad.dtype)], axis=0)
    half_cols = (N_EXPERT // 2) * CAP

    def per_expert(total_dx, scan_items):
        row_table, route_table, gate_matrix, up_matrix, down_matrix = scan_items
        gate_sum = jnp.zeros((D, F), jnp.float32)
        up_sum = jnp.zeros((D, F), jnp.float32)
        down_sum = jnp.zeros((F, D), jnp.float32)
        for group_id in range(N_DP):
            group_gate = jnp.zeros((D, F), jnp.float32)
            group_up = jnp.zeros((D, F), jnp.float32)
            group_down = jnp.zeros((F, D), jnp.float32)
            for lower, upper in ((0, half_cols), (half_cols, N_EXPERT * CAP)):
                row_index = row_table[group_id][lower:upper]
                pair_grad, gate_part, up_part, down_part = swiglu_grads(
                    padded_tokens[row_index], padded_grads[row_index],
                    route_table[group_id][lower:upper].astype(jnp.bfloat16), gate_matrix, up_matrix, down_matrix)
                rounded = lax.optimization_barrier(pair_grad.astype(jnp.bfloat16))
                total_dx = total_dx.at[row_index].add(rounded.astype(jnp.float32), mode="drop")
                gate_kept = lax.optimization_barrier(gate_part.astype(jnp.bfloat16))
                up_kept = lax.optimization_barrier(up_part.astype(jnp.bfloat16))
                down_kept = lax.optimization_barrier(down_part.astype(jnp.bfloat16))
                group_gate = group_gate + gate_kept.astype(jnp.float32)
                group_up = group_up + up_kept.astype(jnp.float32)
                group_down = group_down + down_kept.astype(jnp.float32)
            gate_round = lax.optimization_barrier(group_gate.astype(jnp.bfloat16))
            up_round = lax.optimization_barrier(group_up.astype(jnp.bfloat16))
            down_round = lax.optimization_barrier(group_down.astype(jnp.bfloat16))
            gate_sum = gate_sum + gate_round.astype(jnp.float32)
            up_sum = up_sum + up_round.astype(jnp.float32)
            down_sum = down_sum + down_round.astype(jnp.float32)
        factor = 1.0 / N_DP
        return total_dx, ((gate_sum * factor).astype(jnp.bfloat16), (up_sum * factor).astype(jnp.bfloat16), (down_sum * factor).astype(jnp.bfloat16))

    start_dx = jnp.zeros((token_total, D), jnp.float32)
    total_dx, grad_stack = lax.scan(per_expert, start_dx, (slot_table, weight_table, gate_weight, up_weight, down_weight))
    grad_input = total_dx.astype(jnp.bfloat16)
    return grad_input, grad_stack[0], grad_stack[1], grad_stack[2], expert_load
```

```python
import functools

import jax
import jax.numpy as jnp
from jax import lax
from jax.experimental import pallas as pl
from jax.experimental.pallas import tpu as pltpu
from jax.sharding import PartitionSpec as P

MESH = pl.DeviceIdType.MESH
CAP = 24
SIDE = 4
N_EXPERT = 32
N_DP = 4


def expert_index(z, x, core):
    return ((z % SIDE) * SIDE + x % SIDE) * 2 + core


def remote(src, dst, send_sem, recv_sem, **where):
    return pltpu.make_async_remote_copy(
        src_ref=src, dst_ref=dst, send_sem=send_sem, recv_sem=recv_sem,
        device_id=where, device_id_type=MESH,
    )


def routing_tables(ids_ref, route_ref, sums_ref):
    shape = (N_EXPERT, 8, 128)
    row = lax.broadcasted_iota(jnp.int32, shape, 1)
    expert = lax.broadcasted_iota(jnp.int32, shape, 0) * 2 + row % 2
    count = jnp.zeros(shape, jnp.float32)
    weight = jnp.zeros(shape, jnp.float32)
    for k in range(8):
        hit = expert == ids_ref[k:k + 1, :][None]
        count = count + jnp.where(hit, 1.0, 0.0)
        weight = weight + jnp.where(hit, route_ref[k:k + 1, :][None], 0.0)
    before = lax.broadcasted_iota(jnp.int32, (128, 128), 0) < lax.broadcasted_iota(jnp.int32, (128, 128), 1)
    earlier = jnp.dot(
        count.reshape(N_EXPERT * 8, 128).astype(jnp.bfloat16),
        jnp.where(before, 1.0, 0.0).astype(jnp.bfloat16),
        preferred_element_type=jnp.float32,
    ).reshape(shape)
    slot = jnp.where(count > 0.5, earlier, -1.0)
    sums = jnp.broadcast_to(sums_ref[0:1, :][None], shape)
    return jnp.where(row < 2, slot, jnp.where(row < 4, weight, sums))


OFFSETS = (0, -1, 1, 2)
GROUPS = (
    ((0, 0), (1, 0), (-1, 0), (0, 1)),
    ((0, -1), (2, 0), (0, 2), (1, 1)),
    ((1, -1), (-1, 1), (-1, -1), (1, 2)),
    ((-1, 2), (2, 1), (2, -1), (2, 2)),
)
NT = (((1,), (1,)), ((), ()))
TN = (((0,), (0,)), ((), ()))


def dot(a, b, dims=(((1,), (0,)), ((), ()))):
    return lax.dot_general(a, b, dims, preferred_element_type=jnp.float32)


def offset_slot(d):
    return OFFSETS.index(d)


def pick_rows(meta_all, chip, weighted):
    slots = lax.broadcasted_iota(jnp.int32, (CAP, 128), 0).astype(jnp.float32)
    empty = jnp.zeros((CAP, 128), jnp.float32)
    rows = []
    for e in range(2):
        for b in range(2):
            hit = slots == meta_all[2 * chip + b, e:e + 1, :]
            value = meta_all[2 * chip + b, 2 + e:3 + e, :] if weighted else 1.0
            block = jnp.where(hit, value, 0.0)
            rows.append(jnp.concatenate([block, empty] if b == 0 else [empty, block], axis=1))
    return jnp.concatenate(rows, axis=0).astype(jnp.bfloat16)


def forward_kernel(
    ids_ref, route_ref, sums_ref, tok_hbm, grad_hbm, gate_hbm, up_hbm, down_hbm,
    x_hbm, s_hbm, gu_out, h_out, mine_hbm, theirs_hbm, plane_out,
    tok_all, grad_all, meta_all, meta_send, gate, up, down, xg, sg, nat, pg, stage,
    msend, mrecv, send_sems, recv_sems, dense_send, dense_recv, dense_local, local_sems,
):
    me = lax.axis_index("expert")
    z, x, core = me // (2 * SIDE), (me // 2) % SIDE, me % 2
    pair = expert_index(z, x, 1 - core)

    barrier = pltpu.get_barrier_semaphore()

    def greet(i, _):
        pl.semaphore_signal(barrier, inc=1, device_id={"expert": (me + i) % N_EXPERT}, device_id_type=MESH)
        return 0

    lax.fori_loop(1, N_EXPERT, greet, 0)

    def block(all_ref, index, half=None):
        first = (index % 2) * 128
        if half is None:
            return all_ref.at[index // 2, pl.ds(pl.multiple_of(first, 128), 128)]
        return all_ref.at[index // 2, pl.ds(pl.multiple_of(first + 64 * half, 64), 64)]

    own = [
        pltpu.make_async_copy(tok_hbm, block(tok_all, me), local_sems.at[0]),
        pltpu.make_async_copy(grad_hbm, block(grad_all, me), local_sems.at[1]),
    ]
    weights = [
        pltpu.make_async_copy(hbm, vmem, local_sems.at[2 + n])
        for n, (hbm, vmem) in enumerate(((gate_hbm, gate), (up_hbm, up), (down_hbm, down)))
    ]
    for copy in own:
        copy.start()
    meta_send[...] = routing_tables(ids_ref, route_ref, sums_ref)
    meta_all[me] = meta_send[me]
    for copy in own:
        copy.wait()
    pl.semaphore_wait(barrier, N_EXPERT - 1)

    arrays = ((tok_all, 0), (grad_all, 1))
    started = []
    arrived = set()

    def at(order, dp_, dq, c=None):
        c = core if c is None else c
        return expert_index(z + dp_, x + dq, c) if order == 0 else expert_index(z + dq, x + dp_, c)

    def send(order, key, ref, peer):
        copy = remote(ref, ref, send_sems.at[order, key], recv_sems.at[order, key], expert=peer)
        copy.start()
        started.append(copy)

    def arrive(order, key, dst):
        remote(dst, dst, send_sems.at[order, key], recv_sems.at[order, key], expert=pair).wait_recv()


    def first_axis(order, ref):
        send(order, 0, ref, at(order, 1, 0))
        send(order, 2, ref, at(order, -1, 0))

    def second_axis(order, j, ref):
        send(order, 4 + 4 * j, ref, at(order, 0, 1))
        send(order, 6 + 4 * j, ref, at(order, 0, -1))

    def partner(order, j, i, ref):
        send(order, 20 + 4 * j + i, ref, pair)

    def mark(order, dp_, dq):
        arrived.add((order, (dp_, dq) if order == 0 else (dq, dp_)))

    def got_first(order, all_ref, side):
        j = 1 if side == 0 else 2
        index = at(order, OFFSETS[j], 0)
        ref = block(all_ref, index)
        arrive(order, 2 * side, ref)
        send(order, 2 * side + 1, block(all_ref, index, side), at(order, 1 if side == 0 else -1, 0))
        second_axis(order, j, ref)
        partner(order, j, 0, ref)
        mark(order, OFFSETS[j], 0)

    def got_first_far(order, all_ref):
        index = at(order, 2, 0)
        arrive(order, 1, block(all_ref, index, 0))
        arrive(order, 3, block(all_ref, index, 1))
        second_axis(order, 3, block(all_ref, index))
        partner(order, 3, 0, block(all_ref, index))
        mark(order, 2, 0)

    def got_second(order, all_ref, j, side):
        i = 1 if side == 0 else 2
        index = at(order, OFFSETS[j], OFFSETS[i])
        ref = block(all_ref, index)
        arrive(order, 4 + 4 * j + 2 * side, ref)
        send(order, 5 + 4 * j + 2 * side, block(all_ref, index, side), at(order, 0, 1 if side == 0 else -1))
        partner(order, j, i, ref)
        mark(order, OFFSETS[j], OFFSETS[i])

    def got_second_far(order, all_ref, j):
        index = at(order, OFFSETS[j], 2)
        arrive(order, 5 + 4 * j, block(all_ref, index, 0))
        arrive(order, 7 + 4 * j, block(all_ref, index, 1))
        partner(order, j, 3, block(all_ref, index))
        mark(order, OFFSETS[j], 2)

    for all_ref, order in arrays:
        first_axis(order, block(all_ref, me))
    for all_ref, order in arrays:
        second_axis(order, 0, block(all_ref, me))
        mark(order, 0, 0)

    def send_table(i, _):
        peer = (me + i) % N_EXPERT
        remote(meta_send.at[peer], meta_all.at[me], msend.at[i], mrecv.at[i], expert=peer).start()
        return 0

    lax.fori_loop(1, N_EXPERT, send_table, 0)
    for all_ref, order in arrays:
        partner(order, 0, 0, block(all_ref, me))
    for copy in weights:
        copy.start()

    events = []
    for side in (0, 1):
        for all_ref, order in arrays:
            events.append(functools.partial(got_first, order, all_ref, side))
    for side in (0, 1):
        for all_ref, order in arrays:
            events.append(functools.partial(got_second, order, all_ref, 0, side))
    for all_ref, order in arrays:
        events.append(functools.partial(got_first_far, order, all_ref))
    for j in (1, 2):
        for side in (0, 1):
            for all_ref, order in arrays:
                events.append(functools.partial(got_second, order, all_ref, j, side))
    for all_ref, order in arrays:
        events.append(functools.partial(got_second_far, order, all_ref, 0))
    for side in (0, 1):
        for all_ref, order in arrays:
            events.append(functools.partial(got_second, order, all_ref, 3, side))
    for j in (1, 2, 3):
        for all_ref, order in arrays:
            events.append(functools.partial(got_second_far, order, all_ref, j))

    def run_events(count):
        for _ in range(min(count, len(events))):
            events.pop(0)()

    def dispatch(k, dz, dx):
        while not ((0, (dz, dx)) in arrived and (1, (dz, dx)) in arrived):
            events.pop(0)()
        index = expert_index(z + dz, x + dx, 1 - core)
        for all_ref, order in arrays:
            j, i = (offset_slot(dz), offset_slot(dx)) if order == 0 else (offset_slot(dx), offset_slot(dz))
            arrive(order, 20 + 4 * j + i, block(all_ref, index))
        chip = index // 2
        for all_ref, target, weighted in ((tok_all, xg, False), (grad_all, sg, True)):
            pick = pick_rows(meta_all, chip, weighted)

            def columns(n, _, pick=pick, all_ref=all_ref, target=target):
                cols = pl.ds(pl.multiple_of(n * 512, 512), 512)
                rows = dot(pick, all_ref[chip, :, cols]).astype(jnp.bfloat16)
                for e in range(2):
                    target[e, 48 * k:48 * k + 48, cols] = rows[48 * e:48 * e + 48]
                return 0

            lax.fori_loop(0, 4, columns, 0)

    def forward(g):
        def one(e, _):
            rows = xg[e]
            gate_linear = dot(rows, gate[e])
            up_linear = dot(rows, up[e])
            delta_hidden = dot(sg[e], down[e], NT)
            logistic = jax.nn.sigmoid(gate_linear)
            activated = gate_linear * logistic
            place = slice(192 * (g % 2), 192 * (g % 2) + 192)
            nat[e, 2, place] = (activated * up_linear).astype(jnp.bfloat16)
            delta_gate = (delta_hidden * up_linear * logistic * (1.0 + gate_linear * (1.0 - logistic))).astype(jnp.bfloat16)
            delta_up = (delta_hidden * activated).astype(jnp.bfloat16)
            nat[e, 0, place] = delta_gate
            nat[e, 1, place] = delta_up

            def columns(n, _):
                at_n = pl.ds(pl.multiple_of(n * 512, 512), 512)
                pg[e, :, at_n] = dot(delta_gate, gate[e, at_n, :], NT) + dot(delta_up, up[e, at_n, :], NT)
                return 0

            lax.fori_loop(0, 4, columns, 0)
            return 0

        return one

    dense = []

    def combine(k, dz, dx):
        chip = expert_index(z + dz, x + dx, 0) // 2
        n_dense = len(dense)
        if n_dense >= 2:
            for copy in dense[n_dense - 2]:
                copy()
        pick = pick_rows(meta_all, chip, False)
        here = n_dense % 2

        def columns(n, _):
            cols = pl.ds(pl.multiple_of(n * 512, 512), 512)
            rows = jnp.concatenate([pg[0, 48 * k:48 * k + 48, cols], pg[1, 48 * k:48 * k + 48, cols]], axis=0)
            stage[here, :, cols] = dot(pick, rows.astype(jnp.bfloat16), TN).astype(jnp.bfloat16)
            return 0

        lax.fori_loop(0, 4, columns, 0)
        kept = pltpu.make_async_copy(
            stage.at[here, pl.ds(pl.multiple_of(core * 128, 128), 128)], mine_hbm.at[chip], dense_local.at[n_dense])
        given = remote(
            stage.at[here, pl.ds(pl.multiple_of((1 - core) * 128, 128), 128)], theirs_hbm.at[chip],
            dense_send.at[n_dense], dense_recv.at[n_dense], expert=pair)
        kept.start()
        given.start()
        dense.append((kept.wait, given.wait_send))

    tables_here = []

    def tables():
        def got_table(i, _):
            peer = (me + N_EXPERT - i) % N_EXPERT
            remote(meta_send.at[peer], meta_all.at[peer], msend.at[i], mrecv.at[i], expert=peer).wait_recv()
            return 0

        lax.fori_loop(1, N_EXPERT, got_table, 0)

    stores = []
    run_events(4)
    tables()
    for g, chips in enumerate(GROUPS):
        for copy in stores:
            copy.wait()
        for k, (dz, dx) in enumerate(chips):
            dispatch(k, dz, dx)
            run_events(EVENTS_D)
        stores = [
            pltpu.make_async_copy(xg, x_hbm.at[:, pl.ds(192 * g, 192)], local_sems.at[5]),
            pltpu.make_async_copy(sg, s_hbm.at[:, pl.ds(192 * g, 192)], local_sems.at[6]),
        ]
        for copy in stores:
            copy.start()
        if g == 0:
            for copy in weights:
                copy.wait()
        one = forward(g)
        if g < 3:
            for e in range(2):
                one(e, 0)
                run_events(EVENTS_F)
        else:
            lax.fori_loop(0, 2, one, 0)
        for k, (dz, dx) in enumerate(chips):
            combine(k, dz, dx)
            if k % 2:
                run_events(1)
        if g % 2:
            for e in range(2):
                for n, target, first in ((0, gu_out, 0), (1, gu_out, 384), (2, h_out, 0)):
                    flipped = nat[e, n].astype(jnp.float32).T.astype(jnp.bfloat16)
                    target[e, first:first + 384, 384 * (g // 2):384 * (g // 2) + 384] = flipped
    assert not events
    total = jnp.zeros((8, 128), jnp.float32)
    for s in range(N_EXPERT):
        total = total + meta_all[s]
    plane_out[...] = total

    def sent_table(i, _):
        peer = (me + i) % N_EXPERT
        remote(meta_send.at[peer], meta_all.at[me], msend.at[i], mrecv.at[i], expert=peer).wait_send()
        return 0

    lax.fori_loop(1, N_EXPERT, sent_table, 0)
    for copy in stores:
        copy.wait()
    for copy in started:
        copy.wait_send()
    for waits in dense[-2:]:
        for wait in waits:
            wait()
    n_dense = 0
    for chips in GROUPS:
        for dz, dx in chips:
            chip = expert_index(z + dz, x + dx, 0) // 2
            remote(
                theirs_hbm.at[chip], theirs_hbm.at[chip], dense_send.at[n_dense], dense_recv.at[n_dense], expert=pair
            ).wait_recv()
            n_dense += 1


EVENTS_D = 1
EVENTS_F = 1
VMEM_LIMIT = 67_000_000


def forward_pass(ids, routes, sums, tokens, grads, gate, up, down):
    vmem = pl.BlockSpec(memory_space=pltpu.VMEM)
    anywhere = pl.BlockSpec(memory_space=pl.ANY)
    rows, width = tokens.shape
    hidden = gate.shape[2]
    chips = N_EXPERT // 2
    slots = chips * 2 * CAP
    bf16 = jnp.bfloat16
    dma = pltpu.SemaphoreType.DMA
    return pl.pallas_call(
        forward_kernel,
        out_shape=(
            jax.ShapeDtypeStruct((2, slots, width), bf16),
            jax.ShapeDtypeStruct((2, slots, width), bf16),
            jax.ShapeDtypeStruct((2, 2 * hidden, slots), bf16),
            jax.ShapeDtypeStruct((2, hidden, slots), bf16),
            jax.ShapeDtypeStruct((chips, rows, width), bf16),
            jax.ShapeDtypeStruct((chips, rows, width), bf16),
            jax.ShapeDtypeStruct((8, 128), jnp.float32),
        ),
        in_specs=[vmem] * 3 + [anywhere] * 5,
        out_specs=(anywhere, anywhere, vmem, vmem, anywhere, anywhere, vmem),
        scratch_shapes=[
            pltpu.VMEM((chips, 2 * rows, width), bf16),
            pltpu.VMEM((chips, 2 * rows, width), bf16),
            pltpu.VMEM((N_EXPERT, 8, 128), jnp.float32),
            pltpu.VMEM((N_EXPERT, 8, 128), jnp.float32),
            pltpu.VMEM(gate.shape, bf16),
            pltpu.VMEM(up.shape, bf16),
            pltpu.VMEM(down.shape, bf16),
            pltpu.VMEM((2, slots // 4, width), bf16),
            pltpu.VMEM((2, slots // 4, width), bf16),
            pltpu.VMEM((2, 3, slots // 2, hidden), bf16),
            pltpu.VMEM((2, slots // 4, width), jnp.float32),
            pltpu.VMEM((2, 2 * rows, width), bf16),
            dma((N_EXPERT,)), dma((N_EXPERT,)),
            dma((2, 36)), dma((2, 36)),
            dma((chips,)), dma((chips,)), dma((chips,)),
            dma((7,)),
        ],
        compiler_params=pltpu.CompilerParams(collective_id=0, has_side_effects=True, vmem_limit_bytes=VMEM_LIMIT),
        name="forward_pass",
    )(ids, routes, sums, tokens, grads, gate, up, down)


def finish_kernel(
    x_hbm, s_hbm, gu_ref, h_ref, mine_hbm, theirs_hbm, sums_ref,
    gi_out, gu_out, d_out, sums_out,
    xv, sv, blk, theirs, tx_gu, tx_d, far_gu, far_d, rx_gu, rx_d, q_far, q_near, p_far, p_near,
    far_send, far_recv, near_send, near_recv, qf_send, qf_recv, qn_send, qn_recv,
    pf_send, pf_recv, pn_send, pn_recv, ssend, srecv, local_sems,
):
    me = lax.axis_index("expert")
    y = lax.axis_index("dp")
    z, x, core = me // (2 * SIDE), (me // 2) % SIDE, me % 2
    peers = ((y + 1) % N_DP, (y + 3) % N_DP)
    far_y = (y + 2) % N_DP

    barrier = pltpu.get_barrier_semaphore()
    neighbours = [
        expert_index(z + 1, x, core), expert_index(z - 1, x, core),
        expert_index(z, x + 1, core), expert_index(z, x - 1, core),
    ]
    for peer in neighbours:
        pl.semaphore_signal(barrier, inc=1, device_id={"expert": peer}, device_id_type=MESH)
    for peer in (*peers, far_y):
        pl.semaphore_signal(barrier, inc=1, device_id={"dp": peer}, device_id_type=MESH)
    loads = []
    for n, (hbm, vmem) in enumerate(((x_hbm, xv), (s_hbm, sv), (mine_hbm, blk), (theirs_hbm, theirs))):
        load = pltpu.make_async_copy(hbm, vmem, local_sems.at[n])
        load.start()
        loads.append(load)

    started = []

    def send(copy):
        copy.start()
        started.append(copy)

    def weight_slice(slot, e, owner):
        base = pl.multiple_of(owner * 512, 512)

        def columns(n, _):
            cols = pl.ds(pl.multiple_of(base + n * 256, 256), 256)
            tx_gu[slot, e, :, pl.ds(pl.multiple_of(n * 256, 256), 256)] = dot(gu_ref[e], xv[e, :, cols]).astype(jnp.bfloat16)
            return 0

        lax.fori_loop(0, 2, columns, 0)

    def down_slice(slot, e, owner):
        rows = h_ref[e, pl.ds(pl.multiple_of(owner * 96, 96), 96), :]

        def columns(n, _):
            cols = pl.ds(pl.multiple_of(n * 512, 512), 512)
            tx_d[slot, e, :, cols] = dot(rows, sv[e, :, cols]).astype(jnp.bfloat16)
            return 0

        lax.fori_loop(0, 4, columns, 0)

    kinds = ((weight_slice, tx_gu, far_gu, rx_gu), (down_slice, tx_d, far_d, rx_d))

    def at(order, dp_, dq):
        return (expert_index(z + dp_, x + dq, core) if order == 0 else expert_index(z + dq, x + dp_, core)) // 2

    def device(order, dp_, dq):
        return expert_index(z + dp_, x + dq, core) if order == 0 else expert_index(z + dq, x + dp_, core)

    def cols_of(h):
        return pl.ds(1024 * h, 1024)

    top, bottom = pl.ds(0, 64), pl.ds(64, 64)
    parts = (top, bottom)
    whole = pl.ds(0, 128)
    steps = (1, -1)

    loads[0].wait()
    pl.semaphore_wait(barrier, 7)
    for kind, (compute, tx, far, rx) in enumerate(kinds):
        if kind == 1:
            loads[1].wait()
        for side in (0, 1):
            compute(0, side, far_y)
            send(remote(tx.at[0, side], far.at[side], far_send.at[side, kind], far_recv.at[side, kind], dp=peers[side]))
    for n, other in enumerate((*peers, far_y)):
        send(remote(sums_ref, sums_out.at[n], ssend.at[n], srecv.at[n], dp=other))

    loads[2].wait()
    loads[3].wait()

    def add_partner(i, _):
        for r in range(2):
            rows = parts[r]
            blk[i, rows] = (blk[i, rows].astype(jnp.float32) + theirs[i, rows].astype(jnp.float32)).astype(jnp.bfloat16)
        return 0

    lax.fori_loop(0, N_EXPERT // 2, add_partner, 0)
    for j in range(4):
        for h in range(2):
            for side in (0, 1):
                send(remote(
                    blk.at[at(h, OFFSETS[j], 2), parts[side], cols_of(h)], q_far.at[h, j, parts[side]],
                    qf_send.at[h, j, side], qf_recv.at[h, j, side], expert=device(h, 0, steps[side]),
                ))

    for kind, (compute, tx, far, rx) in enumerate(kinds):
        for side in (0, 1):
            compute(1 + side, 1 - side, peers[side])
            send(remote(
                tx.at[1 + side, 1 - side], rx.at[side, 1 - side],
                near_send.at[side, 1 - side, kind], near_recv.at[side, 1 - side, kind], dp=peers[side],
            ))

    def add_into(target, rows_t, cols_t, value, rows_v):
        target[0][target[1], rows_t, cols_t] = (
            target[0][target[1], rows_t, cols_t].astype(jnp.float32) + value[rows_v].astype(jnp.float32)
        ).astype(jnp.bfloat16)

    for j in (3, 1, 2, 0):
        for h in range(2):
            for side in (0, 1):
                piece = q_far.at[h, j, parts[side]]
                remote(piece, piece, qf_send.at[h, j, side], qf_recv.at[h, j, side], expert=device(h, 0, 1)).wait_recv()
                index = at(h, OFFSETS[j], steps[side])
                blk[index, parts[side], cols_of(h)] = (
                    blk[index, parts[side], cols_of(h)].astype(jnp.float32) + q_far[h, j, parts[side]].astype(jnp.float32)
                ).astype(jnp.bfloat16)
                send(remote(
                    blk.at[index, whole, cols_of(h)], q_near.at[h, j, side],
                    qn_send.at[h, j, side], qn_recv.at[h, j, side], expert=device(h, 0, steps[side]),
                ))

    for kind, (compute, tx, far, rx) in enumerate(kinds):
        for side in (0, 1):
            compute(1 + side, side, peers[side])
            piece = far.at[side]
            remote(piece, piece, far_send.at[side, kind], far_recv.at[side, kind], dp=peers[0]).wait_recv()
            tx[1 + side, side] = (
                tx[1 + side, side].astype(jnp.float32) + far[side].astype(jnp.float32)
            ).astype(jnp.bfloat16)
            send(remote(
                tx.at[1 + side, side], rx.at[side, side],
                near_send.at[side, side, kind], near_recv.at[side, side, kind], dp=peers[side],
            ))

    def second_axis_sum(h, j):
        index = at(h, OFFSETS[j], 0)
        for side in (0, 1):
            piece = q_near.at[h, j, side]
            remote(piece, piece, qn_send.at[h, j, side], qn_recv.at[h, j, side], expert=device(h, 0, 1)).wait_recv()
        blk[index, :, cols_of(h)] = (
            blk[index, :, cols_of(h)].astype(jnp.float32)
            + q_near[h, j, 0].astype(jnp.float32) + q_near[h, j, 1].astype(jnp.float32)
        ).astype(jnp.bfloat16)
        return index

    for h in range(2):
        index = second_axis_sum(h, 3)
        for side in (0, 1):
            send(remote(
                blk.at[index, parts[side], cols_of(h)], p_far.at[h, parts[side]],
                pf_send.at[h, side], pf_recv.at[h, side], expert=device(h, steps[side], 0),
            ))
    for side in (0, 1):
        for h in range(2):
            index = second_axis_sum(h, 2 if side == 0 else 1)
            piece = p_far.at[h, parts[side]]
            remote(piece, piece, pf_send.at[h, side], pf_recv.at[h, side], expert=device(h, 1, 0)).wait_recv()
            blk[index, parts[side], cols_of(h)] = (
                blk[index, parts[side], cols_of(h)].astype(jnp.float32) + p_far[h, parts[side]].astype(jnp.float32)
            ).astype(jnp.bfloat16)
            send(remote(
                blk.at[index, whole, cols_of(h)], p_near.at[h, side],
                pn_send.at[h, side], pn_recv.at[h, side], expert=device(h, steps[side], 0),
            ))
    for kind, (compute, tx, far, rx) in enumerate(kinds):
        for e in (0, 1):
            compute(3, e, y)
    for h in range(2):
        index = second_axis_sum(h, 0)
        for side in (0, 1):
            piece = p_near.at[h, side]
            remote(piece, piece, pn_send.at[h, side], pn_recv.at[h, side], expert=device(h, 1, 0)).wait_recv()
        gi_out[:, cols_of(h)] = (
            blk[index, :, cols_of(h)].astype(jnp.float32)
            + p_near[h, 0].astype(jnp.float32) + p_near[h, 1].astype(jnp.float32)
        ).astype(jnp.bfloat16)
    for n in range(3):
        remote(sums_ref, sums_out.at[n], ssend.at[n], srecv.at[n], dp=far_y).wait_recv()
    factor = 1.0 / N_DP
    for kind, (compute, tx, far, rx) in enumerate(kinds):
        out = (gu_out, d_out)[kind]
        for e in (0, 1):
            for side in (0, 1):
                piece = rx.at[side, e]
                remote(piece, piece, near_send.at[side, e, kind], near_recv.at[side, e, kind], dp=far_y).wait_recv()
            out[e] = (
                (tx[3, e].astype(jnp.float32) + rx[0, e].astype(jnp.float32) + rx[1, e].astype(jnp.float32)) * factor
            ).astype(jnp.bfloat16)
    for copy in started:
        copy.wait_send()


def finish(xs, ss, gu, h, mine, theirs, sums):
    vmem = pl.BlockSpec(memory_space=pltpu.VMEM)
    anywhere = pl.BlockSpec(memory_space=pl.ANY)
    bf16 = jnp.bfloat16
    chips, rows, width = mine.shape
    hidden, slots = h.shape[1:]
    wide, deep = (2 * hidden, width // N_DP), (hidden // N_DP, width)
    dma = pltpu.SemaphoreType.DMA
    buf = lambda *shape: pltpu.VMEM(shape, bf16)
    return pl.pallas_call(
        finish_kernel,
        out_shape=(
            jax.ShapeDtypeStruct((rows, width), bf16),
            jax.ShapeDtypeStruct((2, *wide), bf16),
            jax.ShapeDtypeStruct((2, *deep), bf16),
            jax.ShapeDtypeStruct((3, 8, 128), jnp.float32),
        ),
        in_specs=[anywhere, anywhere, vmem, vmem, anywhere, anywhere, vmem],
        out_specs=(vmem,) * 4,
        scratch_shapes=[
            buf(2, slots, width), buf(2, slots, width), buf(chips, rows, width), buf(chips, rows, width),
            buf(4, 2, *wide), buf(4, 2, *deep), buf(2, *wide), buf(2, *deep), buf(2, 2, *wide), buf(2, 2, *deep),
            buf(2, 4, rows, width // 2), buf(2, 4, 2, rows, width // 2),
            buf(2, rows, width // 2), buf(2, 2, rows, width // 2),
            dma((2, 2)), dma((2, 2)), dma((2, 2, 2)), dma((2, 2, 2)),
            dma((2, 4, 2)), dma((2, 4, 2)), dma((2, 4, 2)), dma((2, 4, 2)),
            dma((2, 2)), dma((2, 2)), dma((2, 2)), dma((2, 2)),
            dma((3,)), dma((3,)), dma((4,)),
        ],
        compiler_params=pltpu.CompilerParams(collective_id=1, has_side_effects=True, vmem_limit_bytes=VMEM_LIMIT),
        name="finish",
    )(xs, ss, gu, h, mine, theirs, sums)


def shards(tokens, out_grad, route_weights, expert_ids, gate_weight, up_weight, down_weight):
    rows, width = tokens.shape
    hidden = gate_weight.shape[2]
    num_experts = 2 * N_EXPERT
    routes = route_weights.astype(jnp.float32)
    chosen = expert_ids[:, :, None] == jnp.arange(num_experts, dtype=jnp.int32)
    local = jnp.sum(jnp.where(chosen, routes[:, :, None], 0.0), axis=(0, 1))
    sums = jnp.broadcast_to(jnp.pad(local, (0, 128 - num_experts))[None], (8, 128))
    xs, ss, gu, h, mine, theirs, plane = forward_pass(
        expert_ids.T, routes.T, sums, tokens, out_grad, gate_weight, up_weight, down_weight
    )
    grad_input, gu_sum, grad_down, other_sums = finish(xs, ss, gu, h, mine, theirs, plane)
    grad_gate = gu_sum[:, :hidden].transpose(0, 2, 1)
    grad_up = gu_sum[:, hidden:].transpose(0, 2, 1)
    expert_weight = (plane[4] + other_sums[0, 4] + other_sums[1, 4] + other_sums[2, 4])[:num_experts]
    expert_load = expert_weight * (num_experts / (rows * N_EXPERT * N_DP * 8))
    return grad_input, grad_gate, grad_up, grad_down, expert_load


def solution(mesh):
    return jax.shard_map(
        shards,
        mesh=mesh,
        in_specs=(
            P(("expert", "dp"), None),
            P(("expert", "dp"), None),
            P(("expert", "dp"), None),
            P(("expert", "dp"), None),
            P("expert", None, None),
            P("expert", None, None),
            P("expert", None, None),
        ),
        out_specs=(
            P(("expert", "dp"), None),
            P("expert", "dp", None),
            P("expert", "dp", None),
            P("expert", "dp", None),
            P(),
        ),
        check_vma=False,
    )
```

```python
import functools

import jax
import jax.numpy as jnp
from jax import lax
from jax.experimental import pallas as pl
from jax.experimental.pallas import tpu as pltpu
from jax.sharding import PartitionSpec as P

MESH = pl.DeviceIdType.MESH
CAP = 24
SIDE = 4
N_EXPERT = 32
N_DP = 4


def expert_index(z, x, core):
    return ((z % SIDE) * SIDE + x % SIDE) * 2 + core


def remote(src, dst, send_sem, recv_sem, **where):
    return pltpu.make_async_remote_copy(
        src_ref=src, dst_ref=dst, send_sem=send_sem, recv_sem=recv_sem,
        device_id=where, device_id_type=MESH,
    )


def routing_tables(ids_ref, route_ref, sums_ref):
    shape = (N_EXPERT, 8, 128)
    row = lax.broadcasted_iota(jnp.int32, shape, 1)
    expert = lax.broadcasted_iota(jnp.int32, shape, 0) * 2 + row % 2
    count = jnp.zeros(shape, jnp.float32)
    weight = jnp.zeros(shape, jnp.float32)
    for k in range(8):
        hit = expert == ids_ref[k:k + 1, :][None]
        count = count + jnp.where(hit, 1.0, 0.0)
        weight = weight + jnp.where(hit, route_ref[k:k + 1, :][None], 0.0)
    before = lax.broadcasted_iota(jnp.int32, (128, 128), 0) < lax.broadcasted_iota(jnp.int32, (128, 128), 1)
    earlier = jnp.dot(
        count.reshape(N_EXPERT * 8, 128).astype(jnp.bfloat16),
        jnp.where(before, 1.0, 0.0).astype(jnp.bfloat16),
        preferred_element_type=jnp.float32,
    ).reshape(shape)
    slot = jnp.where(count > 0.5, earlier, -1.0)
    sums = jnp.broadcast_to(sums_ref[0:1, :][None], shape)
    return jnp.where(row < 2, slot, jnp.where(row < 4, weight, sums))


OFFSETS = (0, -1, 1, 2)
GROUPS = (
    ((0, 0), (1, 0), (-1, 0), (0, 1), (0, -1)),
    ((-1, -1), (1, -1), (-1, 1), (1, 1)),
    ((2, 0), (0, 2), (2, -1), (-1, 2)),
    ((2, 1), (1, 2), (2, 2)),
)
PLAN = ((0, 2, 2, 1), (0, 2, 2, 1), (0, 2, 2, 1), (0, 0, 0, 0))
WIDE_D, WIDE_F, WIDE_C = 2048, 2048, 1024
MOST = 48 * 5
NT = (((1,), (1,)), ((), ()))
TN = (((0,), (0,)), ((), ()))


def dot(a, b, dims=(((1,), (0,)), ((), ()))):
    return lax.dot_general(a, b, dims, preferred_element_type=jnp.float32)


def offset_slot(d):
    return OFFSETS.index(d)


def pick_rows(meta_all, chip, weighted):
    slots = lax.broadcasted_iota(jnp.int32, (CAP, 128), 0).astype(jnp.float32)
    empty = jnp.zeros((CAP, 128), jnp.float32)
    rows = []
    for e in range(2):
        for b in range(2):
            hit = slots == meta_all[2 * chip + b, e:e + 1, :]
            value = meta_all[2 * chip + b, 2 + e:3 + e, :] if weighted else 1.0
            block = jnp.where(hit, value, 0.0)
            rows.append(jnp.concatenate([block, empty] if b == 0 else [empty, block], axis=1))
    return jnp.concatenate(rows, axis=0)


def forward_kernel(
    ids_ref, route_ref, sums_ref, tok_hbm, grad_hbm, gate_hbm, up_hbm, down_hbm,
    x_hbm, s_hbm, gu_out, h_out, mine_hbm, theirs_hbm, plane_out,
    tok_all, grad_all, meta_all, meta_send, gate, up, down, xg, sg, nat, pg, stage, flipped_picks,
    msend, mrecv, send_sems, recv_sems, dense_send, dense_recv, dense_local, local_sems,
):
    me = lax.axis_index("expert")
    z, x, core = me // (2 * SIDE), (me // 2) % SIDE, me % 2
    pair = expert_index(z, x, 1 - core)

    barrier = pltpu.get_barrier_semaphore()

    def greet(i, _):
        pl.semaphore_signal(barrier, inc=1, device_id={"expert": (me + i) % N_EXPERT}, device_id_type=MESH)
        return 0

    lax.fori_loop(1, N_EXPERT, greet, 0)

    def block(all_ref, index, half=None):
        first = (index % 2) * 128
        if half is None:
            return all_ref.at[index // 2, pl.ds(pl.multiple_of(first, 128), 128)]
        return all_ref.at[index // 2, pl.ds(pl.multiple_of(first + 64 * half, 64), 64)]

    own = [
        pltpu.make_async_copy(tok_hbm, block(tok_all, me), local_sems.at[0]),
        pltpu.make_async_copy(grad_hbm, block(grad_all, me), local_sems.at[1]),
    ]
    weights = [
        pltpu.make_async_copy(hbm, vmem, local_sems.at[2 + n])
        for n, (hbm, vmem) in enumerate(((gate_hbm, gate), (up_hbm, up), (down_hbm, down)))
    ]
    for copy in own:
        copy.start()
    meta_send[...] = routing_tables(ids_ref, route_ref, sums_ref)
    meta_all[me] = meta_send[me]
    for copy in own:
        copy.wait()
    pl.semaphore_wait(barrier, N_EXPERT - 1)

    arrays = ((tok_all, 0), (grad_all, 1))
    started = []
    arrived = set()

    def at(order, dp_, dq, c=None):
        c = core if c is None else c
        return expert_index(z + dp_, x + dq, c) if order == 0 else expert_index(z + dq, x + dp_, c)

    def send(order, key, ref, peer):
        copy = remote(ref, ref, send_sems.at[order, key], recv_sems.at[order, key], expert=peer)
        copy.start()
        started.append(copy)

    def arrive(order, key, dst):
        remote(dst, dst, send_sems.at[order, key], recv_sems.at[order, key], expert=pair).wait_recv()


    def first_axis(order, ref):
        send(order, 0, ref, at(order, 1, 0))
        send(order, 2, ref, at(order, -1, 0))

    def second_axis(order, j, ref):
        send(order, 4 + 4 * j, ref, at(order, 0, 1))
        send(order, 6 + 4 * j, ref, at(order, 0, -1))

    def partner(order, j, i, ref):
        send(order, 20 + 4 * j + i, ref, pair)

    def mark(order, dp_, dq):
        arrived.add((order, (dp_, dq) if order == 0 else (dq, dp_)))

    def got_first(order, all_ref, side):
        j = 1 if side == 0 else 2
        index = at(order, OFFSETS[j], 0)
        ref = block(all_ref, index)
        arrive(order, 2 * side, ref)
        send(order, 2 * side + 1, block(all_ref, index, side), at(order, 1 if side == 0 else -1, 0))
        second_axis(order, j, ref)
        partner(order, j, 0, ref)
        mark(order, OFFSETS[j], 0)

    def got_first_far(order, all_ref):
        index = at(order, 2, 0)
        arrive(order, 1, block(all_ref, index, 0))
        arrive(order, 3, block(all_ref, index, 1))
        second_axis(order, 3, block(all_ref, index))
        partner(order, 3, 0, block(all_ref, index))
        mark(order, 2, 0)

    def got_second(order, all_ref, j, side):
        i = 1 if side == 0 else 2
        index = at(order, OFFSETS[j], OFFSETS[i])
        ref = block(all_ref, index)
        arrive(order, 4 + 4 * j + 2 * side, ref)
        send(order, 5 + 4 * j + 2 * side, block(all_ref, index, side), at(order, 0, 1 if side == 0 else -1))
        partner(order, j, i, ref)
        mark(order, OFFSETS[j], OFFSETS[i])

    def got_second_far(order, all_ref, j):
        index = at(order, OFFSETS[j], 2)
        arrive(order, 5 + 4 * j, block(all_ref, index, 0))
        arrive(order, 7 + 4 * j, block(all_ref, index, 1))
        partner(order, j, 3, block(all_ref, index))
        mark(order, OFFSETS[j], 2)

    for all_ref, order in arrays:
        first_axis(order, block(all_ref, me))
    for all_ref, order in arrays:
        second_axis(order, 0, block(all_ref, me))
        mark(order, 0, 0)

    def send_table(i, _):
        peer = (me + i) % N_EXPERT
        remote(meta_send.at[peer], meta_all.at[me], msend.at[i], mrecv.at[i], expert=peer).start()
        return 0

    lax.fori_loop(1, N_EXPERT, send_table, 0)
    for all_ref, order in arrays:
        partner(order, 0, 0, block(all_ref, me))
    for copy in weights:
        copy.start()

    events = []
    for side in (0, 1):
        for all_ref, order in arrays:
            events.append(functools.partial(got_first, order, all_ref, side))
    for side in (0, 1):
        for all_ref, order in arrays:
            events.append(functools.partial(got_second, order, all_ref, 0, side))
    for all_ref, order in arrays:
        events.append(functools.partial(got_first_far, order, all_ref))
    for j in (1, 2):
        for side in (0, 1):
            for all_ref, order in arrays:
                events.append(functools.partial(got_second, order, all_ref, j, side))
    for all_ref, order in arrays:
        events.append(functools.partial(got_second_far, order, all_ref, 0))
    for side in (0, 1):
        for all_ref, order in arrays:
            events.append(functools.partial(got_second, order, all_ref, 3, side))
    for j in (1, 2, 3):
        for all_ref, order in arrays:
            events.append(functools.partial(got_second_far, order, all_ref, j))

    def run_events(count):
        for _ in range(min(count, len(events))):
            events.pop(0)()

    def dispatch(unit, k, dz, dx):
        while not ((0, (dz, dx)) in arrived and (1, (dz, dx)) in arrived):
            events.pop(0)()
        index = expert_index(z + dz, x + dx, 1 - core)
        for all_ref, order in arrays:
            j, i = (offset_slot(dz), offset_slot(dx)) if order == 0 else (offset_slot(dx), offset_slot(dz))
            arrive(order, 20 + 4 * j + i, block(all_ref, index))
        chip = index // 2
        for all_ref, target, weighted in ((tok_all, xg, False), (grad_all, sg, True)):
            pick = pick_rows(meta_all, chip, weighted)
            if not weighted:
                flat = jnp.concatenate([pick, jnp.zeros((32, 256), jnp.float32)], axis=0)
                flipped_picks[unit] = flat.T.astype(jnp.bfloat16)
            pick = pick.astype(jnp.bfloat16)

            def columns(n, _, pick=pick, all_ref=all_ref, target=target):
                cols = pl.ds(pl.multiple_of(n * WIDE_D, WIDE_D), WIDE_D)
                rows = dot(pick, all_ref[chip, :, cols]).astype(jnp.bfloat16)
                for e in range(2):
                    target[e, 48 * k:48 * k + 48, cols] = rows[48 * e:48 * e + 48]
                return 0

            lax.fori_loop(0, 2048 // WIDE_D, columns, 0)

    def forward(first, count):
        place = slice(first, first + count)

        def one(e, _):
            rows = xg[e, 0:count]
            gate_linear = dot(rows, gate[e])
            up_linear = dot(rows, up[e])
            delta_hidden = dot(sg[e, 0:count], down[e], NT)
            logistic = jax.nn.sigmoid(gate_linear)
            activated = gate_linear * logistic
            nat[e, 2, place] = (activated * up_linear).astype(jnp.bfloat16)
            delta_gate = (delta_hidden * up_linear * logistic * (1.0 + gate_linear * (1.0 - logistic))).astype(jnp.bfloat16)
            delta_up = (delta_hidden * activated).astype(jnp.bfloat16)
            nat[e, 0, place] = delta_gate
            nat[e, 1, place] = delta_up

            def columns(n, _):
                at_n = pl.ds(pl.multiple_of(n * WIDE_F, WIDE_F), WIDE_F)
                pg[e, 0:count, at_n] = dot(delta_gate, gate[e, at_n, :], NT) + dot(delta_up, up[e, at_n, :], NT)
                return 0

            lax.fori_loop(0, 2048 // WIDE_F, columns, 0)
            return 0

        return one

    dense = []

    def combine(k, dz, dx):
        chip = expert_index(z + dz, x + dx, 0) // 2
        n_dense = len(dense)
        if n_dense >= 2:
            for copy in dense[n_dense - 2]:
                copy()
        here = n_dense % 2
        empty = jnp.zeros((32, WIDE_C), jnp.float32)

        def columns(n, _):
            cols = pl.ds(pl.multiple_of(n * WIDE_C, WIDE_C), WIDE_C)
            rows = jnp.concatenate([pg[0, 48 * k:48 * k + 48, cols], pg[1, 48 * k:48 * k + 48, cols], empty], axis=0)
            stage[here, :, cols] = dot(flipped_picks[n_dense], rows.astype(jnp.bfloat16)).astype(jnp.bfloat16)
            return 0

        lax.fori_loop(0, 2048 // WIDE_C, columns, 0)
        kept = pltpu.make_async_copy(
            stage.at[here, pl.ds(pl.multiple_of(core * 128, 128), 128)], mine_hbm.at[chip], dense_local.at[n_dense])
        given = remote(
            stage.at[here, pl.ds(pl.multiple_of((1 - core) * 128, 128), 128)], theirs_hbm.at[chip],
            dense_send.at[n_dense], dense_recv.at[n_dense], expert=pair)
        kept.start()
        given.start()
        dense.append((kept.wait, given.wait_send))

    tables_here = []

    def tables():
        def got_table(i, _):
            peer = (me + N_EXPERT - i) % N_EXPERT
            remote(meta_send.at[peer], meta_all.at[peer], msend.at[i], mrecv.at[i], expert=peer).wait_recv()
            return 0

        lax.fori_loop(1, N_EXPERT, got_table, 0)

    stores = []
    run_events(4)
    tables()
    first = 0
    for g, chips in enumerate(GROUPS):
        count = 48 * len(chips)
        after_dispatch, after_one, after_two, after_combine = PLAN[g]
        for copy in stores:
            copy.wait()
        for k, (dz, dx) in enumerate(chips):
            dispatch(first // 48 + k, k, dz, dx)
            run_events(after_dispatch)
        stores = [
            pltpu.make_async_copy(xg.at[:, pl.ds(0, count)], x_hbm.at[:, pl.ds(first, count)], local_sems.at[5]),
            pltpu.make_async_copy(sg.at[:, pl.ds(0, count)], s_hbm.at[:, pl.ds(first, count)], local_sems.at[6]),
        ]
        for copy in stores:
            copy.start()
        if g == 0:
            for copy in weights:
                copy.wait()
        one = forward(first, count)
        if g < 3:
            one(0, 0)
            run_events(after_one)
            one(1, 0)
            run_events(after_two)
        else:
            lax.fori_loop(0, 2, one, 0)
        for k, (dz, dx) in enumerate(chips):
            combine(k, dz, dx)
            run_events(after_combine)
        first += count
        if g >= 2:
            begin, end = ((0, 512), (512, 768))[g - 2]
            for e in range(2):
                for n, target, row in ((0, gu_out, 0), (1, gu_out, 384), (2, h_out, 0)):
                    flipped = nat[e, n, begin:end].astype(jnp.float32).T.astype(jnp.bfloat16)
                    target[e, row:row + 384, begin:end] = flipped
    assert not events
    total = jnp.zeros((8, 128), jnp.float32)
    for s in range(N_EXPERT):
        total = total + meta_all[s]
    plane_out[...] = total

    def sent_table(i, _):
        peer = (me + i) % N_EXPERT
        remote(meta_send.at[peer], meta_all.at[me], msend.at[i], mrecv.at[i], expert=peer).wait_send()
        return 0

    lax.fori_loop(1, N_EXPERT, sent_table, 0)
    for copy in stores:
        copy.wait()
    for copy in started:
        copy.wait_send()
    for waits in dense[-2:]:
        for wait in waits:
            wait()
    n_dense = 0
    for chips in GROUPS:
        for dz, dx in chips:
            chip = expert_index(z + dz, x + dx, 0) // 2
            remote(
                theirs_hbm.at[chip], theirs_hbm.at[chip], dense_send.at[n_dense], dense_recv.at[n_dense], expert=pair
            ).wait_recv()
            n_dense += 1


VMEM_LIMIT = 67_000_000


def forward_pass(ids, routes, sums, tokens, grads, gate, up, down):
    vmem = pl.BlockSpec(memory_space=pltpu.VMEM)
    anywhere = pl.BlockSpec(memory_space=pl.ANY)
    rows, width = tokens.shape
    hidden = gate.shape[2]
    chips = N_EXPERT // 2
    slots = chips * 2 * CAP
    bf16 = jnp.bfloat16
    dma = pltpu.SemaphoreType.DMA
    return pl.pallas_call(
        forward_kernel,
        out_shape=(
            jax.ShapeDtypeStruct((2, slots, width), bf16),
            jax.ShapeDtypeStruct((2, slots, width), bf16),
            jax.ShapeDtypeStruct((2, 2 * hidden, slots), bf16),
            jax.ShapeDtypeStruct((2, hidden, slots), bf16),
            jax.ShapeDtypeStruct((chips, rows, width), bf16),
            jax.ShapeDtypeStruct((chips, rows, width), bf16),
            jax.ShapeDtypeStruct((8, 128), jnp.float32),
        ),
        in_specs=[vmem] * 3 + [anywhere] * 5,
        out_specs=(anywhere, anywhere, vmem, vmem, anywhere, anywhere, vmem),
        scratch_shapes=[
            pltpu.VMEM((chips, 2 * rows, width), bf16),
            pltpu.VMEM((chips, 2 * rows, width), bf16),
            pltpu.VMEM((N_EXPERT, 8, 128), jnp.float32),
            pltpu.VMEM((N_EXPERT, 8, 128), jnp.float32),
            pltpu.VMEM(gate.shape, bf16),
            pltpu.VMEM(up.shape, bf16),
            pltpu.VMEM(down.shape, bf16),
            pltpu.VMEM((2, MOST, width), bf16),
            pltpu.VMEM((2, MOST, width), bf16),
            pltpu.VMEM((2, 3, slots, hidden), bf16),
            pltpu.VMEM((2, MOST, width), jnp.float32),
            pltpu.VMEM((2, 2 * rows, width), bf16),
            pltpu.VMEM((chips, 2 * rows, 128), bf16),
            dma((N_EXPERT,)), dma((N_EXPERT,)),
            dma((2, 36)), dma((2, 36)),
            dma((chips,)), dma((chips,)), dma((chips,)),
            dma((7,)),
        ],
        compiler_params=pltpu.CompilerParams(collective_id=0, has_side_effects=True, vmem_limit_bytes=VMEM_LIMIT),
        name="forward_pass",
    )(ids, routes, sums, tokens, grads, gate, up, down)


def finish_kernel(
    x_hbm, s_hbm, gu_ref, h_ref, mine_hbm, theirs_hbm, sums_ref,
    gi_out, gu_out, d_out, sums_out,
    xv, sv, blk, theirs, tx_gu, tx_d, far_gu, far_d, rx_gu, rx_d, q_far, q_near, p_far, p_near,
    far_send, far_recv, near_send, near_recv, qf_send, qf_recv, qn_send, qn_recv,
    pf_send, pf_recv, pn_send, pn_recv, ssend, srecv, local_sems,
):
    me = lax.axis_index("expert")
    y = lax.axis_index("dp")
    z, x, core = me // (2 * SIDE), (me // 2) % SIDE, me % 2
    peers = ((y + 1) % N_DP, (y + 3) % N_DP)
    far_y = (y + 2) % N_DP

    barrier = pltpu.get_barrier_semaphore()
    neighbours = [
        expert_index(z + 1, x, core), expert_index(z - 1, x, core),
        expert_index(z, x + 1, core), expert_index(z, x - 1, core),
    ]
    for peer in neighbours:
        pl.semaphore_signal(barrier, inc=1, device_id={"expert": peer}, device_id_type=MESH)
    for peer in (*peers, far_y):
        pl.semaphore_signal(barrier, inc=1, device_id={"dp": peer}, device_id_type=MESH)
    loads = []
    for n, (hbm, vmem) in enumerate(((x_hbm, xv), (s_hbm, sv), (mine_hbm, blk), (theirs_hbm, theirs))):
        load = pltpu.make_async_copy(hbm, vmem, local_sems.at[n])
        load.start()
        loads.append(load)

    started = []

    def send(copy):
        copy.start()
        started.append(copy)

    def weight_slice(slot, e, owner):
        base = pl.multiple_of(owner * 512, 512)

        def columns(n, _):
            cols = pl.ds(pl.multiple_of(base + n * 256, 256), 256)
            tx_gu[slot, e, :, pl.ds(pl.multiple_of(n * 256, 256), 256)] = dot(gu_ref[e], xv[e, :, cols]).astype(jnp.bfloat16)
            return 0

        lax.fori_loop(0, 2, columns, 0)

    def down_slice(slot, e, owner):
        rows = h_ref[e, pl.ds(pl.multiple_of(owner * 96, 96), 96), :]

        def columns(n, _):
            cols = pl.ds(pl.multiple_of(n * 512, 512), 512)
            tx_d[slot, e, :, cols] = dot(rows, sv[e, :, cols]).astype(jnp.bfloat16)
            return 0

        lax.fori_loop(0, 4, columns, 0)

    kinds = ((weight_slice, tx_gu, far_gu, rx_gu), (down_slice, tx_d, far_d, rx_d))

    def at(order, dp_, dq):
        return (expert_index(z + dp_, x + dq, core) if order == 0 else expert_index(z + dq, x + dp_, core)) // 2

    def device(order, dp_, dq):
        return expert_index(z + dp_, x + dq, core) if order == 0 else expert_index(z + dq, x + dp_, core)

    def cols_of(h):
        return pl.ds(1024 * h, 1024)

    top, bottom = pl.ds(0, 64), pl.ds(64, 64)
    parts = (top, bottom)
    whole = pl.ds(0, 128)
    steps = (1, -1)

    loads[0].wait()
    pl.semaphore_wait(barrier, 7)
    for kind, (compute, tx, far, rx) in enumerate(kinds):
        if kind == 1:
            loads[1].wait()
        for side in (0, 1):
            compute(0, side, far_y)
            send(remote(tx.at[0, side], far.at[side], far_send.at[side, kind], far_recv.at[side, kind], dp=peers[side]))
    for n, other in enumerate((*peers, far_y)):
        send(remote(sums_ref, sums_out.at[n], ssend.at[n], srecv.at[n], dp=other))

    loads[2].wait()
    loads[3].wait()

    def add_partner(i, _):
        for r in range(2):
            rows = parts[r]
            blk[i, rows] = (blk[i, rows].astype(jnp.float32) + theirs[i, rows].astype(jnp.float32)).astype(jnp.bfloat16)
        return 0

    lax.fori_loop(0, N_EXPERT // 2, add_partner, 0)
    for j in range(4):
        for h in range(2):
            for side in (0, 1):
                send(remote(
                    blk.at[at(h, OFFSETS[j], 2), parts[side], cols_of(h)], q_far.at[h, j, parts[side]],
                    qf_send.at[h, j, side], qf_recv.at[h, j, side], expert=device(h, 0, steps[side]),
                ))

    for kind, (compute, tx, far, rx) in enumerate(kinds):
        for side in (0, 1):
            compute(1 + side, 1 - side, peers[side])
            send(remote(
                tx.at[1 + side, 1 - side], rx.at[side, 1 - side],
                near_send.at[side, 1 - side, kind], near_recv.at[side, 1 - side, kind], dp=peers[side],
            ))

    def add_into(target, rows_t, cols_t, value, rows_v):
        target[0][target[1], rows_t, cols_t] = (
            target[0][target[1], rows_t, cols_t].astype(jnp.float32) + value[rows_v].astype(jnp.float32)
        ).astype(jnp.bfloat16)

    for j in (3, 1, 2, 0):
        for h in range(2):
            for side in (0, 1):
                piece = q_far.at[h, j, parts[side]]
                remote(piece, piece, qf_send.at[h, j, side], qf_recv.at[h, j, side], expert=device(h, 0, 1)).wait_recv()
                index = at(h, OFFSETS[j], steps[side])
                blk[index, parts[side], cols_of(h)] = (
                    blk[index, parts[side], cols_of(h)].astype(jnp.float32) + q_far[h, j, parts[side]].astype(jnp.float32)
                ).astype(jnp.bfloat16)
                send(remote(
                    blk.at[index, whole, cols_of(h)], q_near.at[h, j, side],
                    qn_send.at[h, j, side], qn_recv.at[h, j, side], expert=device(h, 0, steps[side]),
                ))

    for kind, (compute, tx, far, rx) in enumerate(kinds):
        for side in (0, 1):
            compute(1 + side, side, peers[side])
            piece = far.at[side]
            remote(piece, piece, far_send.at[side, kind], far_recv.at[side, kind], dp=peers[0]).wait_recv()
            tx[1 + side, side] = (
                tx[1 + side, side].astype(jnp.float32) + far[side].astype(jnp.float32)
            ).astype(jnp.bfloat16)
            send(remote(
                tx.at[1 + side, side], rx.at[side, side],
                near_send.at[side, side, kind], near_recv.at[side, side, kind], dp=peers[side],
            ))

    def second_axis_sum(h, j):
        index = at(h, OFFSETS[j], 0)
        for side in (0, 1):
            piece = q_near.at[h, j, side]
            remote(piece, piece, qn_send.at[h, j, side], qn_recv.at[h, j, side], expert=device(h, 0, 1)).wait_recv()
        blk[index, :, cols_of(h)] = (
            blk[index, :, cols_of(h)].astype(jnp.float32)
            + q_near[h, j, 0].astype(jnp.float32) + q_near[h, j, 1].astype(jnp.float32)
        ).astype(jnp.bfloat16)
        return index

    for h in range(2):
        index = second_axis_sum(h, 3)
        for side in (0, 1):
            send(remote(
                blk.at[index, parts[side], cols_of(h)], p_far.at[h, parts[side]],
                pf_send.at[h, side], pf_recv.at[h, side], expert=device(h, steps[side], 0),
            ))
    for side in (0, 1):
        for h in range(2):
            index = second_axis_sum(h, 2 if side == 0 else 1)
            piece = p_far.at[h, parts[side]]
            remote(piece, piece, pf_send.at[h, side], pf_recv.at[h, side], expert=device(h, 1, 0)).wait_recv()
            blk[index, parts[side], cols_of(h)] = (
                blk[index, parts[side], cols_of(h)].astype(jnp.float32) + p_far[h, parts[side]].astype(jnp.float32)
            ).astype(jnp.bfloat16)
            send(remote(
                blk.at[index, whole, cols_of(h)], p_near.at[h, side],
                pn_send.at[h, side], pn_recv.at[h, side], expert=device(h, steps[side], 0),
            ))
    for kind, (compute, tx, far, rx) in enumerate(kinds):
        for e in (0, 1):
            compute(3, e, y)
    for h in range(2):
        index = second_axis_sum(h, 0)
        for side in (0, 1):
            piece = p_near.at[h, side]
            remote(piece, piece, pn_send.at[h, side], pn_recv.at[h, side], expert=device(h, 1, 0)).wait_recv()
        gi_out[:, cols_of(h)] = (
            blk[index, :, cols_of(h)].astype(jnp.float32)
            + p_near[h, 0].astype(jnp.float32) + p_near[h, 1].astype(jnp.float32)
        ).astype(jnp.bfloat16)
    for n in range(3):
        remote(sums_ref, sums_out.at[n], ssend.at[n], srecv.at[n], dp=far_y).wait_recv()
    factor = 1.0 / N_DP
    for kind, (compute, tx, far, rx) in enumerate(kinds):
        out = (gu_out, d_out)[kind]
        for e in (0, 1):
            for side in (0, 1):
                piece = rx.at[side, e]
                remote(piece, piece, near_send.at[side, e, kind], near_recv.at[side, e, kind], dp=far_y).wait_recv()
            out[e] = (
                (tx[3, e].astype(jnp.float32) + rx[0, e].astype(jnp.float32) + rx[1, e].astype(jnp.float32)) * factor
            ).astype(jnp.bfloat16)
    for copy in started:
        copy.wait_send()


def finish(xs, ss, gu, h, mine, theirs, sums):
    vmem = pl.BlockSpec(memory_space=pltpu.VMEM)
    anywhere = pl.BlockSpec(memory_space=pl.ANY)
    bf16 = jnp.bfloat16
    chips, rows, width = mine.shape
    hidden, slots = h.shape[1:]
    wide, deep = (2 * hidden, width // N_DP), (hidden // N_DP, width)
    dma = pltpu.SemaphoreType.DMA
    buf = lambda *shape: pltpu.VMEM(shape, bf16)
    return pl.pallas_call(
        finish_kernel,
        out_shape=(
            jax.ShapeDtypeStruct((rows, width), bf16),
            jax.ShapeDtypeStruct((2, *wide), bf16),
            jax.ShapeDtypeStruct((2, *deep), bf16),
            jax.ShapeDtypeStruct((3, 8, 128), jnp.float32),
        ),
        in_specs=[anywhere, anywhere, vmem, vmem, anywhere, anywhere, vmem],
        out_specs=(vmem,) * 4,
        scratch_shapes=[
            buf(2, slots, width), buf(2, slots, width), buf(chips, rows, width), buf(chips, rows, width),
            buf(4, 2, *wide), buf(4, 2, *deep), buf(2, *wide), buf(2, *deep), buf(2, 2, *wide), buf(2, 2, *deep),
            buf(2, 4, rows, width // 2), buf(2, 4, 2, rows, width // 2),
            buf(2, rows, width // 2), buf(2, 2, rows, width // 2),
            dma((2, 2)), dma((2, 2)), dma((2, 2, 2)), dma((2, 2, 2)),
            dma((2, 4, 2)), dma((2, 4, 2)), dma((2, 4, 2)), dma((2, 4, 2)),
            dma((2, 2)), dma((2, 2)), dma((2, 2)), dma((2, 2)),
            dma((3,)), dma((3,)), dma((4,)),
        ],
        compiler_params=pltpu.CompilerParams(collective_id=1, has_side_effects=True, vmem_limit_bytes=VMEM_LIMIT),
        name="finish",
    )(xs, ss, gu, h, mine, theirs, sums)


def shards(tokens, out_grad, route_weights, expert_ids, gate_weight, up_weight, down_weight):
    rows, width = tokens.shape
    hidden = gate_weight.shape[2]
    num_experts = 2 * N_EXPERT
    routes = route_weights.astype(jnp.float32)
    chosen = expert_ids[:, :, None] == jnp.arange(num_experts, dtype=jnp.int32)
    local = jnp.sum(jnp.where(chosen, routes[:, :, None], 0.0), axis=(0, 1))
    sums = jnp.broadcast_to(jnp.pad(local, (0, 128 - num_experts))[None], (8, 128))
    xs, ss, gu, h, mine, theirs, plane = forward_pass(
        expert_ids.T, routes.T, sums, tokens, out_grad, gate_weight, up_weight, down_weight
    )
    grad_input, gu_sum, grad_down, other_sums = finish(xs, ss, gu, h, mine, theirs, plane)
    grad_gate = gu_sum[:, :hidden].transpose(0, 2, 1)
    grad_up = gu_sum[:, hidden:].transpose(0, 2, 1)
    expert_weight = (plane[4] + other_sums[0, 4] + other_sums[1, 4] + other_sums[2, 4])[:num_experts]
    expert_load = expert_weight * (num_experts / (rows * N_EXPERT * N_DP * 8))
    return grad_input, grad_gate, grad_up, grad_down, expert_load


def solution(mesh):
    return jax.shard_map(
        shards,
        mesh=mesh,
        in_specs=(
            P(("expert", "dp"), None),
            P(("expert", "dp"), None),
            P(("expert", "dp"), None),
            P(("expert", "dp"), None),
            P("expert", None, None),
            P("expert", None, None),
            P("expert", None, None),
        ),
        out_specs=(
            P(("expert", "dp"), None),
            P("expert", "dp", None),
            P("expert", "dp", None),
            P("expert", "dp", None),
            P(),
        ),
        check_vma=False,
    )
```

```python
import functools

import jax
import jax.numpy as jnp
from jax import lax
from jax.experimental import pallas as pl
from jax.experimental.pallas import tpu as pltpu
from jax.sharding import PartitionSpec as P

MESH = pl.DeviceIdType.MESH
CAP = 24
SIDE = 4
N_EXPERT = 32
N_DP = 4


def expert_index(z, x, core):
    return ((z % SIDE) * SIDE + x % SIDE) * 2 + core


def remote(src, dst, send_sem, recv_sem, **where):
    return pltpu.make_async_remote_copy(
        src_ref=src, dst_ref=dst, send_sem=send_sem, recv_sem=recv_sem,
        device_id=where, device_id_type=MESH,
    )


def routing_tables(ids_ref, route_ref):
    shape = (N_EXPERT, 8, 128)
    row = lax.broadcasted_iota(jnp.int32, shape, 1)
    expert = lax.broadcasted_iota(jnp.int32, shape, 0) * 2 + row % 2
    count = jnp.zeros(shape, jnp.float32)
    weight = jnp.zeros(shape, jnp.float32)
    for k in range(8):
        hit = expert == ids_ref[k:k + 1, :][None]
        count = count + jnp.where(hit, 1.0, 0.0)
        weight = weight + jnp.where(hit, route_ref[k:k + 1, :][None], 0.0)
    before = lax.broadcasted_iota(jnp.int32, (128, 128), 0) < lax.broadcasted_iota(jnp.int32, (128, 128), 1)
    earlier = jnp.dot(
        count.reshape(N_EXPERT * 8, 128).astype(jnp.bfloat16),
        jnp.where(before, 1.0, 0.0).astype(jnp.bfloat16),
        preferred_element_type=jnp.float32,
    ).reshape(shape)
    slot = jnp.where(count > 0.5, earlier, -1.0)
    expert = lax.broadcasted_iota(jnp.int32, (128, 128), 0)
    weights = jnp.zeros((128, 128), jnp.float32)
    for k in range(8):
        weights = weights + jnp.where(expert == ids_ref[k:k + 1, :], route_ref[k:k + 1, :], 0.0)
    local = lax.dot_general(
        jnp.ones((8, 128), jnp.bfloat16), weights.astype(jnp.bfloat16), (((1,), (1,)), ((), ())),
        preferred_element_type=jnp.float32,
    )
    sums = jnp.broadcast_to(local[None], shape)
    return jnp.where(row < 2, slot, jnp.where(row < 4, weight, sums))


OFFSETS = (0, -1, 1, 2)
GROUPS = (
    ((0, 0), (1, 0), (-1, 0), (0, 1), (0, -1)),
    ((-1, -1), (1, -1), (-1, 1), (1, 1)),
    ((2, 0), (0, 2), (2, -1), (-1, 2)),
    ((2, 1), (1, 2), (2, 2)),
)
PLAN = ((0, 2, 2, 1), (0, 2, 2, 1), (0, 2, 2, 1), (0, 0, 0, 0))
WIDE_D, WIDE_F, WIDE_C = 2048, 2048, 1024
MOST = 48 * 5
NT = (((1,), (1,)), ((), ()))
TN = (((0,), (0,)), ((), ()))


def dot(a, b, dims=(((1,), (0,)), ((), ()))):
    return lax.dot_general(a, b, dims, preferred_element_type=jnp.float32)


def offset_slot(d):
    return OFFSETS.index(d)


def pick_rows(meta_all, chip, weighted):
    slots = lax.broadcasted_iota(jnp.int32, (CAP, 128), 0).astype(jnp.float32)
    empty = jnp.zeros((CAP, 128), jnp.float32)
    rows = []
    for e in range(2):
        for b in range(2):
            hit = slots == meta_all[2 * chip + b, e:e + 1, :]
            value = meta_all[2 * chip + b, 2 + e:3 + e, :] if weighted else 1.0
            block = jnp.where(hit, value, 0.0)
            rows.append(jnp.concatenate([block, empty] if b == 0 else [empty, block], axis=1))
    return jnp.concatenate(rows, axis=0)


def forward_kernel(
    ids_ref, route_ref, tok_hbm, grad_hbm, gate_hbm, up_hbm, down_hbm,
    x_hbm, s_hbm, gu_hbm, h_out, mine_hbm, theirs_hbm, plane_out,
    tok_all, grad_all, meta_all, meta_send, gate, up, down, xg, sg, deltas, hid, pg, stage, flipped_picks,
    msend, mrecv, send_sems, recv_sems, dense_send, dense_recv, dense_local, local_sems,
):
    me = lax.axis_index("expert")
    z, x, core = me // (2 * SIDE), (me // 2) % SIDE, me % 2
    pair = expert_index(z, x, 1 - core)

    barrier = pltpu.get_barrier_semaphore()

    def greet(i, _):
        pl.semaphore_signal(barrier, inc=1, device_id={"expert": (me + i) % N_EXPERT}, device_id_type=MESH)
        return 0

    lax.fori_loop(1, N_EXPERT, greet, 0)

    def block(all_ref, index, half=None):
        first = (index % 2) * 128
        if half is None:
            return all_ref.at[index // 2, pl.ds(pl.multiple_of(first, 128), 128)]
        return all_ref.at[index // 2, pl.ds(pl.multiple_of(first + 64 * half, 64), 64)]

    own = [
        pltpu.make_async_copy(tok_hbm, block(tok_all, me), local_sems.at[0]),
        pltpu.make_async_copy(grad_hbm, block(grad_all, me), local_sems.at[1]),
    ]
    weights = [
        pltpu.make_async_copy(hbm, vmem, local_sems.at[2 + n])
        for n, (hbm, vmem) in enumerate(((gate_hbm, gate), (up_hbm, up), (down_hbm, down)))
    ]
    for copy in own:
        copy.start()
    meta_send[...] = routing_tables(ids_ref, route_ref)
    meta_all[me] = meta_send[me]
    for copy in own:
        copy.wait()
    pl.semaphore_wait(barrier, N_EXPERT - 1)

    arrays = ((tok_all, 0), (grad_all, 1))
    started = []
    arrived = set()

    def at(order, dp_, dq, c=None):
        c = core if c is None else c
        return expert_index(z + dp_, x + dq, c) if order == 0 else expert_index(z + dq, x + dp_, c)

    def send(order, key, ref, peer):
        copy = remote(ref, ref, send_sems.at[order, key], recv_sems.at[order, key], expert=peer)
        copy.start()
        started.append(copy)

    def arrive(order, key, dst):
        remote(dst, dst, send_sems.at[order, key], recv_sems.at[order, key], expert=pair).wait_recv()


    def first_axis(order, ref):
        send(order, 0, ref, at(order, 1, 0))
        send(order, 2, ref, at(order, -1, 0))

    def second_axis(order, j, ref):
        send(order, 4 + 4 * j, ref, at(order, 0, 1))
        send(order, 6 + 4 * j, ref, at(order, 0, -1))

    def partner(order, j, i, ref):
        send(order, 20 + 4 * j + i, ref, pair)

    def mark(order, dp_, dq):
        arrived.add((order, (dp_, dq) if order == 0 else (dq, dp_)))

    def got_first(order, all_ref, side):
        j = 1 if side == 0 else 2
        index = at(order, OFFSETS[j], 0)
        ref = block(all_ref, index)
        arrive(order, 2 * side, ref)
        send(order, 2 * side + 1, block(all_ref, index, side), at(order, 1 if side == 0 else -1, 0))
        second_axis(order, j, ref)
        partner(order, j, 0, ref)
        mark(order, OFFSETS[j], 0)

    def got_first_far(order, all_ref):
        index = at(order, 2, 0)
        arrive(order, 1, block(all_ref, index, 0))
        arrive(order, 3, block(all_ref, index, 1))
        second_axis(order, 3, block(all_ref, index))
        partner(order, 3, 0, block(all_ref, index))
        mark(order, 2, 0)

    def got_second(order, all_ref, j, side):
        i = 1 if side == 0 else 2
        index = at(order, OFFSETS[j], OFFSETS[i])
        ref = block(all_ref, index)
        arrive(order, 4 + 4 * j + 2 * side, ref)
        send(order, 5 + 4 * j + 2 * side, block(all_ref, index, side), at(order, 0, 1 if side == 0 else -1))
        partner(order, j, i, ref)
        mark(order, OFFSETS[j], OFFSETS[i])

    def got_second_far(order, all_ref, j):
        index = at(order, OFFSETS[j], 2)
        arrive(order, 5 + 4 * j, block(all_ref, index, 0))
        arrive(order, 7 + 4 * j, block(all_ref, index, 1))
        partner(order, j, 3, block(all_ref, index))
        mark(order, OFFSETS[j], 2)

    for all_ref, order in arrays:
        first_axis(order, block(all_ref, me))
    for all_ref, order in arrays:
        second_axis(order, 0, block(all_ref, me))
        mark(order, 0, 0)

    def send_table(i, _):
        peer = (me + i) % N_EXPERT
        remote(meta_send.at[peer], meta_all.at[me], msend.at[i], mrecv.at[i], expert=peer).start()
        return 0

    lax.fori_loop(1, N_EXPERT, send_table, 0)
    for all_ref, order in arrays:
        partner(order, 0, 0, block(all_ref, me))
    for copy in weights:
        copy.start()

    events = []
    for side in (0, 1):
        for all_ref, order in arrays:
            events.append(functools.partial(got_first, order, all_ref, side))
    for side in (0, 1):
        for all_ref, order in arrays:
            events.append(functools.partial(got_second, order, all_ref, 0, side))
    for all_ref, order in arrays:
        events.append(functools.partial(got_first_far, order, all_ref))
    for j in (1, 2):
        for side in (0, 1):
            for all_ref, order in arrays:
                events.append(functools.partial(got_second, order, all_ref, j, side))
    for all_ref, order in arrays:
        events.append(functools.partial(got_second_far, order, all_ref, 0))
    for side in (0, 1):
        for all_ref, order in arrays:
            events.append(functools.partial(got_second, order, all_ref, 3, side))
    for j in (1, 2, 3):
        for all_ref, order in arrays:
            events.append(functools.partial(got_second_far, order, all_ref, j))

    def run_events(count):
        for _ in range(min(count, len(events))):
            events.pop(0)()

    def dispatch(unit, k, dz, dx):
        while not ((0, (dz, dx)) in arrived and (1, (dz, dx)) in arrived):
            events.pop(0)()
        index = expert_index(z + dz, x + dx, 1 - core)
        for all_ref, order in arrays:
            j, i = (offset_slot(dz), offset_slot(dx)) if order == 0 else (offset_slot(dx), offset_slot(dz))
            arrive(order, 20 + 4 * j + i, block(all_ref, index))
        chip = index // 2
        for all_ref, target, weighted in ((tok_all, xg, False), (grad_all, sg, True)):
            pick = pick_rows(meta_all, chip, weighted)
            if not weighted:
                flat = jnp.concatenate([pick, jnp.zeros((32, 256), jnp.float32)], axis=0)
                flipped_picks[unit] = flat.T.astype(jnp.bfloat16)
            pick = pick.astype(jnp.bfloat16)

            def columns(n, _, pick=pick, all_ref=all_ref, target=target):
                cols = pl.ds(pl.multiple_of(n * WIDE_D, WIDE_D), WIDE_D)
                rows = dot(pick, all_ref[chip, :, cols]).astype(jnp.bfloat16)
                for e in range(2):
                    target[e, 48 * k:48 * k + 48, cols] = rows[48 * e:48 * e + 48]
                return 0

            lax.fori_loop(0, 2048 // WIDE_D, columns, 0)

    def forward(first, count):
        place = slice(first, first + count)

        def one(e, _):
            rows = xg[e, 0:count]
            gate_linear = dot(rows, gate[e])
            up_linear = dot(rows, up[e])
            delta_hidden = dot(sg[e, 0:count], down[e], NT)
            logistic = jax.nn.sigmoid(gate_linear)
            activated = gate_linear * logistic
            hid[e, place] = (activated * up_linear).astype(jnp.bfloat16)
            delta_gate = (delta_hidden * up_linear * logistic * (1.0 + gate_linear * (1.0 - logistic))).astype(jnp.bfloat16)
            delta_up = (delta_hidden * activated).astype(jnp.bfloat16)
            deltas[e, place, 0:384] = delta_gate
            deltas[e, place, 384:768] = delta_up

            def columns(n, _):
                at_n = pl.ds(pl.multiple_of(n * WIDE_F, WIDE_F), WIDE_F)
                pg[e, 0:count, at_n] = dot(delta_gate, gate[e, at_n, :], NT) + dot(delta_up, up[e, at_n, :], NT)
                return 0

            lax.fori_loop(0, 2048 // WIDE_F, columns, 0)
            return 0

        return one

    dense = []

    def combine(k, dz, dx):
        chip = expert_index(z + dz, x + dx, 0) // 2
        n_dense = len(dense)
        if n_dense >= 2:
            for copy in dense[n_dense - 2]:
                copy()
        here = n_dense % 2
        empty = jnp.zeros((32, WIDE_C), jnp.float32)

        def columns(n, _):
            cols = pl.ds(pl.multiple_of(n * WIDE_C, WIDE_C), WIDE_C)
            rows = jnp.concatenate([pg[0, 48 * k:48 * k + 48, cols], pg[1, 48 * k:48 * k + 48, cols], empty], axis=0)
            stage[here, :, cols] = dot(flipped_picks[n_dense], rows.astype(jnp.bfloat16)).astype(jnp.bfloat16)
            return 0

        lax.fori_loop(0, 2048 // WIDE_C, columns, 0)
        kept = pltpu.make_async_copy(
            stage.at[here, pl.ds(pl.multiple_of(core * 128, 128), 128)], mine_hbm.at[chip], dense_local.at[n_dense])
        given = remote(
            stage.at[here, pl.ds(pl.multiple_of((1 - core) * 128, 128), 128)], theirs_hbm.at[chip],
            dense_send.at[n_dense], dense_recv.at[n_dense], expert=pair)
        kept.start()
        given.start()
        dense.append((kept.wait, given.wait_send))

    tables_here = []

    def tables():
        def got_table(i, _):
            peer = (me + N_EXPERT - i) % N_EXPERT
            remote(meta_send.at[peer], meta_all.at[peer], msend.at[i], mrecv.at[i], expert=peer).wait_recv()
            return 0

        lax.fori_loop(1, N_EXPERT, got_table, 0)

    stores, kept_deltas = [], []
    run_events(4)
    tables()
    first = 0
    for g, chips in enumerate(GROUPS):
        count = 48 * len(chips)
        after_dispatch, after_one, after_two, after_combine = PLAN[g]
        for copy in stores:
            copy.wait()
        for k, (dz, dx) in enumerate(chips):
            dispatch(first // 48 + k, k, dz, dx)
            run_events(after_dispatch)
        stores = [
            pltpu.make_async_copy(xg.at[:, pl.ds(0, count)], x_hbm.at[:, pl.ds(first, count)], local_sems.at[5]),
            pltpu.make_async_copy(sg.at[:, pl.ds(0, count)], s_hbm.at[:, pl.ds(first, count)], local_sems.at[6]),
        ]
        for copy in stores:
            copy.start()
        if g == 0:
            for copy in weights:
                copy.wait()
        one = forward(first, count)
        if g < 3:
            one(0, 0)
            run_events(after_one)
            one(1, 0)
            run_events(after_two)
        else:
            lax.fori_loop(0, 2, one, 0)
        keep = pltpu.make_async_copy(
            deltas.at[:, pl.ds(first, count)], gu_hbm.at[:, pl.ds(first, count)], local_sems.at[7 + g])
        keep.start()
        kept_deltas.append(keep)
        for k, (dz, dx) in enumerate(chips):
            combine(k, dz, dx)
            run_events(after_combine)
        first += count
        if g >= 2:
            begin, end = ((0, 512), (512, 768))[g - 2]
            for e in range(2):
                h_out[e, :, begin:end] = hid[e, begin:end].astype(jnp.float32).T.astype(jnp.bfloat16)
    assert not events
    total = jnp.zeros((8, 128), jnp.float32)
    for s in range(N_EXPERT):
        total = total + meta_all[s]
    plane_out[...] = total

    def sent_table(i, _):
        peer = (me + i) % N_EXPERT
        remote(meta_send.at[peer], meta_all.at[me], msend.at[i], mrecv.at[i], expert=peer).wait_send()
        return 0

    lax.fori_loop(1, N_EXPERT, sent_table, 0)
    for copy in stores + kept_deltas:
        copy.wait()
    for copy in started:
        copy.wait_send()
    for waits in dense[-2:]:
        for wait in waits:
            wait()
    n_dense = 0
    for chips in GROUPS:
        for dz, dx in chips:
            chip = expert_index(z + dz, x + dx, 0) // 2
            remote(
                theirs_hbm.at[chip], theirs_hbm.at[chip], dense_send.at[n_dense], dense_recv.at[n_dense], expert=pair
            ).wait_recv()
            n_dense += 1


VMEM_LIMIT = 67_000_000
LOAD_SCALE = 2 * N_EXPERT / (N_EXPERT * N_DP * 128 * 8)


def forward_pass(ids, routes, tokens, grads, gate, up, down):
    vmem = pl.BlockSpec(memory_space=pltpu.VMEM)
    anywhere = pl.BlockSpec(memory_space=pl.ANY)
    rows, width = tokens.shape
    hidden = gate.shape[2]
    chips = N_EXPERT // 2
    slots = chips * 2 * CAP
    bf16 = jnp.bfloat16
    dma = pltpu.SemaphoreType.DMA
    return pl.pallas_call(
        forward_kernel,
        out_shape=(
            jax.ShapeDtypeStruct((2, slots, width), bf16),
            jax.ShapeDtypeStruct((2, slots, width), bf16),
            jax.ShapeDtypeStruct((2, slots, 2 * hidden), bf16),
            jax.ShapeDtypeStruct((2, hidden, slots), bf16),
            jax.ShapeDtypeStruct((chips, rows, width), bf16),
            jax.ShapeDtypeStruct((chips, rows, width), bf16),
            jax.ShapeDtypeStruct((8, 128), jnp.float32),
        ),
        in_specs=[vmem] * 2 + [anywhere] * 5,
        out_specs=(anywhere, anywhere, anywhere, vmem, anywhere, anywhere, vmem),
        scratch_shapes=[
            pltpu.VMEM((chips, 2 * rows, width), bf16),
            pltpu.VMEM((chips, 2 * rows, width), bf16),
            pltpu.VMEM((N_EXPERT, 8, 128), jnp.float32),
            pltpu.VMEM((N_EXPERT, 8, 128), jnp.float32),
            pltpu.VMEM(gate.shape, bf16),
            pltpu.VMEM(up.shape, bf16),
            pltpu.VMEM(down.shape, bf16),
            pltpu.VMEM((2, MOST, width), bf16),
            pltpu.VMEM((2, MOST, width), bf16),
            pltpu.VMEM((2, slots, 2 * hidden), bf16),
            pltpu.VMEM((2, slots, hidden), bf16),
            pltpu.VMEM((2, MOST, width), jnp.float32),
            pltpu.VMEM((2, 2 * rows, width), bf16),
            pltpu.VMEM((chips, 2 * rows, 128), bf16),
            dma((N_EXPERT,)), dma((N_EXPERT,)),
            dma((2, 36)), dma((2, 36)),
            dma((chips,)), dma((chips,)), dma((chips,)),
            dma((11,)),
        ],
        compiler_params=pltpu.CompilerParams(collective_id=0, has_side_effects=True, vmem_limit_bytes=VMEM_LIMIT),
        name="forward_pass",
    )(ids, routes, tokens, grads, gate, up, down)


def finish_kernel(
    x_hbm, s_hbm, gu_hbm, h_hbm, mine_hbm, theirs_hbm, sums_ref,
    gi_out, gate_out, up_out, d_out, load_out,
    xv, sv, deltas, hid, sums_out, blk, theirs, tx_gu, tx_d, far_gu, far_d, rx_gu, rx_d, q_far, q_near, p_far, p_near,
    far_send, far_recv, near_send, near_recv, qf_send, qf_recv, qn_send, qn_recv,
    pf_send, pf_recv, pn_send, pn_recv, ssend, srecv, local_sems,
):
    me = lax.axis_index("expert")
    y = lax.axis_index("dp")
    z, x, core = me // (2 * SIDE), (me // 2) % SIDE, me % 2
    peers = ((y + 1) % N_DP, (y + 3) % N_DP)
    far_y = (y + 2) % N_DP

    barrier = pltpu.get_barrier_semaphore()
    neighbours = [
        expert_index(z + 1, x, core), expert_index(z - 1, x, core),
        expert_index(z, x + 1, core), expert_index(z, x - 1, core),
    ]
    for peer in neighbours:
        pl.semaphore_signal(barrier, inc=1, device_id={"expert": peer}, device_id_type=MESH)
    for peer in (*peers, far_y):
        pl.semaphore_signal(barrier, inc=1, device_id={"dp": peer}, device_id_type=MESH)
    loads = []
    for n, (hbm, vmem) in enumerate((
        (x_hbm.at[0], xv.at[0]), (gu_hbm.at[0], deltas.at[0]), (x_hbm.at[1], xv.at[1]), (gu_hbm.at[1], deltas.at[1]),
        (s_hbm, sv), (h_hbm, hid), (mine_hbm, blk), (theirs_hbm, theirs),
    )):
        load = pltpu.make_async_copy(hbm, vmem, local_sems.at[n])
        load.start()
        loads.append(load)

    started = []

    def send(copy):
        copy.start()
        started.append(copy)

    def weight_slice(slot, e, owner):
        base = pl.multiple_of(owner * 512, 512)

        def columns(n, _):
            cols = pl.ds(pl.multiple_of(base + n * 256, 256), 256)
            rows = pl.ds(pl.multiple_of(n * 256, 256), 256)
            tx_gu[slot, e, rows] = dot(xv[e, :, cols], deltas[e], TN).astype(jnp.bfloat16)
            return 0

        lax.fori_loop(0, 2, columns, 0)

    def down_slice(slot, e, owner):
        rows = hid[e, pl.ds(pl.multiple_of(owner * 96, 96), 96), :]

        def columns(n, _):
            cols = pl.ds(pl.multiple_of(n * 1024, 1024), 1024)
            tx_d[slot, e, :, cols] = dot(rows, sv[e, :, cols]).astype(jnp.bfloat16)
            return 0

        lax.fori_loop(0, 2, columns, 0)

    def by_rows(first, count, body):
        def step(i, _):
            body(pl.ds(pl.multiple_of(first + i * 32, 32), 32))
            return 0

        lax.fori_loop(0, count // 32, step, 0)

    def wide(value):
        return value.astype(jnp.float32)

    kinds = ((weight_slice, tx_gu, far_gu, rx_gu), (down_slice, tx_d, far_d, rx_d))

    def at(order, dp_, dq):
        return (expert_index(z + dp_, x + dq, core) if order == 0 else expert_index(z + dq, x + dp_, core)) // 2

    def device(order, dp_, dq):
        return expert_index(z + dp_, x + dq, core) if order == 0 else expert_index(z + dq, x + dp_, core)

    def cols_of(h):
        return pl.ds(1024 * h, 1024)

    top, bottom = pl.ds(0, 64), pl.ds(64, 64)
    parts = (top, bottom)
    whole = pl.ds(0, 128)
    steps = (1, -1)

    for kind, (compute, tx, far, rx) in enumerate(kinds):
        for side in (0, 1):
            for load in loads[2 * side:2 * side + 2] if kind == 0 else loads[4:6] if side == 0 else ():
                load.wait()
            compute(0, side, far_y)
            if kind == 0 and side == 0:
                pl.semaphore_wait(barrier, 7)
            send(remote(tx.at[0, side], far.at[side], far_send.at[side, kind], far_recv.at[side, kind], dp=peers[side]))
    for n, other in enumerate((*peers, far_y)):
        send(remote(sums_ref, sums_out.at[n], ssend.at[n], srecv.at[n], dp=other))

    loads[6].wait()
    loads[7].wait()

    def add_partner(i, _):
        chip = i // 4
        rows = pl.ds(pl.multiple_of(i % 4 * 32, 32), 32)
        blk[chip, rows] = (wide(blk[chip, rows]) + wide(theirs[chip, rows])).astype(jnp.bfloat16)
        return 0

    lax.fori_loop(0, N_EXPERT * 2, add_partner, 0)
    for j in range(4):
        for h in range(2):
            for side in (0, 1):
                send(remote(
                    blk.at[at(h, OFFSETS[j], 2), parts[side], cols_of(h)], q_far.at[h, j, parts[side]],
                    qf_send.at[h, j, side], qf_recv.at[h, j, side], expert=device(h, 0, steps[side]),
                ))

    for kind, (compute, tx, far, rx) in enumerate(kinds):
        for side in (0, 1):
            compute(1 + side, 1 - side, peers[side])
            send(remote(
                tx.at[1 + side, 1 - side], rx.at[side, 1 - side],
                near_send.at[side, 1 - side, kind], near_recv.at[side, 1 - side, kind], dp=peers[side],
            ))

    for j in (3, 1, 2, 0):
        for h in range(2):
            for side in (0, 1):
                piece = q_far.at[h, j, parts[side]]
                remote(piece, piece, qf_send.at[h, j, side], qf_recv.at[h, j, side], expert=device(h, 0, 1)).wait_recv()
                index = at(h, OFFSETS[j], steps[side])

                def add_far(rows, index=index, h=h, j=j):
                    blk[index, rows, cols_of(h)] = (
                        wide(blk[index, rows, cols_of(h)]) + wide(q_far[h, j, rows])).astype(jnp.bfloat16)

                by_rows(64 * side, 64, add_far)
                send(remote(
                    blk.at[index, whole, cols_of(h)], q_near.at[h, j, side],
                    qn_send.at[h, j, side], qn_recv.at[h, j, side], expert=device(h, 0, steps[side]),
                ))

    for kind, (compute, tx, far, rx) in enumerate(kinds):
        for side in (0, 1):
            compute(1 + side, side, peers[side])
            piece = far.at[side]
            remote(piece, piece, far_send.at[side, kind], far_recv.at[side, kind], dp=peers[0]).wait_recv()

            def add_far(rows, tx=tx, far=far, side=side):
                tx[1 + side, side, rows] = (wide(tx[1 + side, side, rows]) + wide(far[side, rows])).astype(jnp.bfloat16)

            by_rows(0, tx.shape[2], add_far)
            send(remote(
                tx.at[1 + side, side], rx.at[side, side],
                near_send.at[side, side, kind], near_recv.at[side, side, kind], dp=peers[side],
            ))

    def second_axis_sum(h, j):
        index = at(h, OFFSETS[j], 0)
        for side in (0, 1):
            piece = q_near.at[h, j, side]
            remote(piece, piece, qn_send.at[h, j, side], qn_recv.at[h, j, side], expert=device(h, 0, 1)).wait_recv()

        def add_near(rows):
            blk[index, rows, cols_of(h)] = (
                wide(blk[index, rows, cols_of(h)]) + wide(q_near[h, j, 0, rows]) + wide(q_near[h, j, 1, rows])
            ).astype(jnp.bfloat16)

        by_rows(0, 128, add_near)
        return index

    for h in range(2):
        index = second_axis_sum(h, 3)
        for side in (0, 1):
            send(remote(
                blk.at[index, parts[side], cols_of(h)], p_far.at[h, parts[side]],
                pf_send.at[h, side], pf_recv.at[h, side], expert=device(h, steps[side], 0),
            ))
    for side in (0, 1):
        for h in range(2):
            index = second_axis_sum(h, 2 if side == 0 else 1)
            piece = p_far.at[h, parts[side]]
            remote(piece, piece, pf_send.at[h, side], pf_recv.at[h, side], expert=device(h, 1, 0)).wait_recv()

            def add_far(rows, index=index, h=h):
                blk[index, rows, cols_of(h)] = (
                    wide(blk[index, rows, cols_of(h)]) + wide(p_far[h, rows])).astype(jnp.bfloat16)

            by_rows(64 * side, 64, add_far)
            send(remote(
                blk.at[index, whole, cols_of(h)], p_near.at[h, side],
                pn_send.at[h, side], pn_recv.at[h, side], expert=device(h, steps[side], 0),
            ))
    for kind, (compute, tx, far, rx) in enumerate(kinds):
        for e in (0, 1):
            compute(3, e, y)
    for h in range(2):
        index = second_axis_sum(h, 0)
        for side in (0, 1):
            piece = p_near.at[h, side]
            remote(piece, piece, pn_send.at[h, side], pn_recv.at[h, side], expert=device(h, 1, 0)).wait_recv()

        def add_last(rows, index=index, h=h):
            gi_out[rows, cols_of(h)] = (
                wide(blk[index, rows, cols_of(h)]) + wide(p_near[h, 0, rows]) + wide(p_near[h, 1, rows])
            ).astype(jnp.bfloat16)

        by_rows(0, 128, add_last)
    for n in range(3):
        remote(sums_ref, sums_out.at[n], ssend.at[n], srecv.at[n], dp=far_y).wait_recv()
    load_out[...] = (sums_ref[...] + sums_out[0] + sums_out[1] + sums_out[2]) * LOAD_SCALE
    factor = 1.0 / N_DP
    for kind, (compute, tx, far, rx) in enumerate(kinds):
        for e in (0, 1):
            for side in (0, 1):
                piece = rx.at[side, e]
                remote(piece, piece, near_send.at[side, e, kind], near_recv.at[side, e, kind], dp=far_y).wait_recv()

            def total(rows, kind=kind, e=e, tx=tx, rx=rx):
                value = ((wide(tx[3, e, rows]) + wide(rx[0, e, rows]) + wide(rx[1, e, rows])) * factor).astype(jnp.bfloat16)
                if kind == 0:
                    gate_out[e, rows] = value[:, 0:384]
                    up_out[e, rows] = value[:, 384:768]
                else:
                    d_out[e, rows] = value

            by_rows(0, tx.shape[2], total)
    for copy in started:
        copy.wait_send()


def finish(xs, ss, gu, h, mine, theirs, sums):
    vmem = pl.BlockSpec(memory_space=pltpu.VMEM)
    anywhere = pl.BlockSpec(memory_space=pl.ANY)
    bf16 = jnp.bfloat16
    chips, rows, width = mine.shape
    hidden, slots = h.shape[1:]
    tile = (8, 128)
    wide, deep = (width // N_DP, 2 * hidden), (hidden // N_DP, width)
    near = (2, width // N_DP, hidden)
    dma = pltpu.SemaphoreType.DMA
    buf = lambda *shape: pltpu.VMEM(shape, bf16)
    return pl.pallas_call(
        finish_kernel,
        out_shape=(
            jax.ShapeDtypeStruct((rows, width), bf16),
            jax.ShapeDtypeStruct(near, bf16),
            jax.ShapeDtypeStruct(near, bf16),
            jax.ShapeDtypeStruct((2, *deep), bf16),
            jax.ShapeDtypeStruct(tile, jnp.float32),
        ),
        in_specs=[anywhere] * 6 + [vmem],
        out_specs=(vmem,) * 5,
        scratch_shapes=[
            buf(2, slots, width), buf(2, slots, width), buf(2, slots, 2 * hidden), buf(2, hidden, slots),
            pltpu.VMEM((3, *tile), jnp.float32), buf(chips, rows, width), buf(chips, rows, width),
            buf(4, 2, *wide), buf(4, 2, *deep), buf(2, *wide), buf(2, *deep), buf(2, 2, *wide), buf(2, 2, *deep),
            buf(2, 4, rows, width // 2), buf(2, 4, 2, rows, width // 2),
            buf(2, rows, width // 2), buf(2, 2, rows, width // 2),
            dma((2, 2)), dma((2, 2)), dma((2, 2, 2)), dma((2, 2, 2)),
            dma((2, 4, 2)), dma((2, 4, 2)), dma((2, 4, 2)), dma((2, 4, 2)),
            dma((2, 2)), dma((2, 2)), dma((2, 2)), dma((2, 2)),
            dma((3,)), dma((3,)), dma((8,)),
        ],
        compiler_params=pltpu.CompilerParams(collective_id=1, has_side_effects=True, vmem_limit_bytes=VMEM_LIMIT),
        name="finish",
    )(xs, ss, gu, h, mine, theirs, sums)


def shards(tokens, out_grad, route_weights, expert_ids, gate_weight, up_weight, down_weight):
    rows, width = tokens.shape
    num_experts = 2 * N_EXPERT
    routes = route_weights.astype(jnp.float32)
    xs, ss, gu, h, mine, theirs, plane = forward_pass(
        expert_ids.T, routes.T, tokens, out_grad, gate_weight, up_weight, down_weight
    )
    grad_input, grad_gate, grad_up, grad_down, load = finish(xs, ss, gu, h, mine, theirs, plane)
    return grad_input, grad_gate, grad_up, grad_down, load[4, :num_experts]


def solution(mesh):
    return jax.shard_map(
        shards,
        mesh=mesh,
        in_specs=(
            P(("expert", "dp"), None),
            P(("expert", "dp"), None),
            P(("expert", "dp"), None),
            P(("expert", "dp"), None),
            P("expert", None, None),
            P("expert", None, None),
            P("expert", None, None),
        ),
        out_specs=(
            P(("expert", "dp"), None),
            P("expert", "dp", None),
            P("expert", "dp", None),
            P("expert", "dp", None),
            P(),
        ),
        check_vma=False,
    )
```

```python
import functools

import jax
import jax.numpy as jnp
from jax import lax
from jax.experimental import pallas as pl
from jax.experimental.pallas import tpu as pltpu
from jax.sharding import PartitionSpec as P

MESH = pl.DeviceIdType.MESH
CAP = 24
SIDE = 4
N_EXPERT = 32
N_DP = 4


def expert_index(z, x, core):
    return ((z % SIDE) * SIDE + x % SIDE) * 2 + core


def remote(src, dst, send_sem, recv_sem, **where):
    return pltpu.make_async_remote_copy(
        src_ref=src, dst_ref=dst, send_sem=send_sem, recv_sem=recv_sem,
        device_id=where, device_id_type=MESH,
    )


def routing_tables(ids_ref, route_ref):
    shape = (N_EXPERT, 8, 128)
    row = lax.broadcasted_iota(jnp.int32, shape, 1)
    expert = lax.broadcasted_iota(jnp.int32, shape, 0) * 2 + row % 2
    count = jnp.zeros(shape, jnp.float32)
    weight = jnp.zeros(shape, jnp.float32)
    for k in range(8):
        hit = expert == ids_ref[k:k + 1, :][None]
        count = count + jnp.where(hit, 1.0, 0.0)
        weight = weight + jnp.where(hit, route_ref[k:k + 1, :][None], 0.0)
    before = lax.broadcasted_iota(jnp.int32, (128, 128), 0) < lax.broadcasted_iota(jnp.int32, (128, 128), 1)
    earlier = jnp.dot(
        count.reshape(N_EXPERT * 8, 128).astype(jnp.bfloat16),
        jnp.where(before, 1.0, 0.0).astype(jnp.bfloat16),
        preferred_element_type=jnp.float32,
    ).reshape(shape)
    slot = jnp.where(count > 0.5, earlier, -1.0)
    expert = lax.broadcasted_iota(jnp.int32, (128, 128), 0)
    weights = jnp.zeros((128, 128), jnp.float32)
    for k in range(8):
        weights = weights + jnp.where(expert == ids_ref[k:k + 1, :], route_ref[k:k + 1, :], 0.0)
    local = lax.dot_general(
        jnp.ones((8, 128), jnp.bfloat16), weights.astype(jnp.bfloat16), (((1,), (1,)), ((), ())),
        preferred_element_type=jnp.float32,
    )
    sums = jnp.broadcast_to(local[None], shape)
    return jnp.where(row < 2, slot, jnp.where(row < 4, weight, sums))


OFFSETS = (0, -1, 1, 2)
GROUPS = (
    ((0, 0), (1, 0), (-1, 0), (0, 1), (0, -1)),
    ((-1, -1), (1, -1), (-1, 1), (1, 1)),
    ((2, 0), (0, 2), (2, -1), (-1, 2)),
    ((2, 1), (1, 2), (2, 2)),
)
PLAN = ((0, 2, 2, 1), (0, 2, 2, 1), (0, 2, 2, 1), (0, 0, 0, 0))
STAGES = 3
WIDE_D, WIDE_F, WIDE_C = 2048, 2048, 1024
MOST = 48 * 5
NT = (((1,), (1,)), ((), ()))
TN = (((0,), (0,)), ((), ()))


def dot(a, b, dims=(((1,), (0,)), ((), ()))):
    return lax.dot_general(a, b, dims, preferred_element_type=jnp.float32)


def offset_slot(d):
    return OFFSETS.index(d)


def pick_rows(meta_all, chip, weighted):
    slots = lax.broadcasted_iota(jnp.int32, (CAP, 128), 0).astype(jnp.float32)
    empty = jnp.zeros((CAP, 128), jnp.float32)
    rows = []
    for e in range(2):
        for b in range(2):
            hit = slots == meta_all[2 * chip + b, e:e + 1, :]
            value = meta_all[2 * chip + b, 2 + e:3 + e, :] if weighted else 1.0
            block = jnp.where(hit, value, 0.0)
            rows.append(jnp.concatenate([block, empty] if b == 0 else [empty, block], axis=1))
    return jnp.concatenate(rows, axis=0)


def forward_kernel(
    ids_ref, route_ref, tok_hbm, grad_hbm, gate_hbm, up_hbm, down_hbm,
    x_hbm, s_hbm, gu_hbm, h_out, mine_hbm, theirs_hbm, plane_out,
    tok_all, grad_all, meta_all, meta_send, gate, up, down, xg, sg, deltas, hid, pg, stage, flipped_picks,
    msend, mrecv, send_sems, recv_sems, dense_send, dense_recv, dense_local, local_sems,
):
    me = lax.axis_index("expert")
    z, x, core = me // (2 * SIDE), (me // 2) % SIDE, me % 2
    pair = expert_index(z, x, 1 - core)

    barrier = pltpu.get_barrier_semaphore()

    def greet(i, _):
        pl.semaphore_signal(barrier, inc=1, device_id={"expert": (me + i) % N_EXPERT}, device_id_type=MESH)
        return 0

    lax.fori_loop(1, N_EXPERT, greet, 0)

    def block(all_ref, index, half=None):
        first = (index % 2) * 128
        if half is None:
            return all_ref.at[index // 2, pl.ds(pl.multiple_of(first, 128), 128)]
        return all_ref.at[index // 2, pl.ds(pl.multiple_of(first + 64 * half, 64), 64)]

    own = [
        pltpu.make_async_copy(tok_hbm, block(tok_all, me), local_sems.at[0]),
        pltpu.make_async_copy(grad_hbm, block(grad_all, me), local_sems.at[1]),
    ]
    weights = [
        pltpu.make_async_copy(hbm, vmem, local_sems.at[2 + n])
        for n, (hbm, vmem) in enumerate(((gate_hbm, gate), (up_hbm, up), (down_hbm, down)))
    ]
    for copy in own:
        copy.start()
    meta_send[...] = routing_tables(ids_ref, route_ref)
    meta_all[me] = meta_send[me]
    for copy in own:
        copy.wait()
    pl.semaphore_wait(barrier, N_EXPERT - 1)

    arrays = ((tok_all, 0), (grad_all, 1))
    started = []
    arrived = set()

    def at(order, dp_, dq, c=None):
        c = core if c is None else c
        return expert_index(z + dp_, x + dq, c) if order == 0 else expert_index(z + dq, x + dp_, c)

    def send(order, key, ref, peer):
        copy = remote(ref, ref, send_sems.at[order, key], recv_sems.at[order, key], expert=peer)
        copy.start()
        started.append(copy)

    def arrive(order, key, dst):
        remote(dst, dst, send_sems.at[order, key], recv_sems.at[order, key], expert=pair).wait_recv()


    def first_axis(order, ref):
        send(order, 0, ref, at(order, 1, 0))
        send(order, 2, ref, at(order, -1, 0))

    def second_axis(order, j, ref):
        send(order, 4 + 4 * j, ref, at(order, 0, 1))
        send(order, 6 + 4 * j, ref, at(order, 0, -1))

    def partner(order, j, i, ref):
        send(order, 20 + 4 * j + i, ref, pair)

    def mark(order, dp_, dq):
        arrived.add((order, (dp_, dq) if order == 0 else (dq, dp_)))

    def got_first(order, all_ref, side):
        j = 1 if side == 0 else 2
        index = at(order, OFFSETS[j], 0)
        ref = block(all_ref, index)
        arrive(order, 2 * side, ref)
        send(order, 2 * side + 1, block(all_ref, index, side), at(order, 1 if side == 0 else -1, 0))
        second_axis(order, j, ref)
        partner(order, j, 0, ref)
        mark(order, OFFSETS[j], 0)

    def got_first_far(order, all_ref):
        index = at(order, 2, 0)
        arrive(order, 1, block(all_ref, index, 0))
        arrive(order, 3, block(all_ref, index, 1))
        second_axis(order, 3, block(all_ref, index))
        partner(order, 3, 0, block(all_ref, index))
        mark(order, 2, 0)

    def got_second(order, all_ref, j, side):
        i = 1 if side == 0 else 2
        index = at(order, OFFSETS[j], OFFSETS[i])
        ref = block(all_ref, index)
        arrive(order, 4 + 4 * j + 2 * side, ref)
        send(order, 5 + 4 * j + 2 * side, block(all_ref, index, side), at(order, 0, 1 if side == 0 else -1))
        partner(order, j, i, ref)
        mark(order, OFFSETS[j], OFFSETS[i])

    def got_second_far(order, all_ref, j):
        index = at(order, OFFSETS[j], 2)
        arrive(order, 5 + 4 * j, block(all_ref, index, 0))
        arrive(order, 7 + 4 * j, block(all_ref, index, 1))
        partner(order, j, 3, block(all_ref, index))
        mark(order, OFFSETS[j], 2)

    for all_ref, order in arrays:
        first_axis(order, block(all_ref, me))
    for all_ref, order in arrays:
        second_axis(order, 0, block(all_ref, me))
        mark(order, 0, 0)

    def send_table(i, _):
        peer = (me + i) % N_EXPERT
        remote(meta_send.at[peer], meta_all.at[me], msend.at[i], mrecv.at[i], expert=peer).start()
        return 0

    lax.fori_loop(1, N_EXPERT, send_table, 0)
    for all_ref, order in arrays:
        partner(order, 0, 0, block(all_ref, me))
    for copy in weights:
        copy.start()

    events = []
    for side in (0, 1):
        for all_ref, order in arrays:
            events.append(functools.partial(got_first, order, all_ref, side))
    for side in (0, 1):
        for all_ref, order in arrays:
            events.append(functools.partial(got_second, order, all_ref, 0, side))
    for all_ref, order in arrays:
        events.append(functools.partial(got_first_far, order, all_ref))
    for j in (1, 2):
        for side in (0, 1):
            for all_ref, order in arrays:
                events.append(functools.partial(got_second, order, all_ref, j, side))
    for all_ref, order in arrays:
        events.append(functools.partial(got_second_far, order, all_ref, 0))
    for side in (0, 1):
        for all_ref, order in arrays:
            events.append(functools.partial(got_second, order, all_ref, 3, side))
    for j in (1, 2, 3):
        for all_ref, order in arrays:
            events.append(functools.partial(got_second_far, order, all_ref, j))

    def run_events(count):
        for _ in range(min(count, len(events))):
            events.pop(0)()

    def dispatch(unit, k, dz, dx):
        while not ((0, (dz, dx)) in arrived and (1, (dz, dx)) in arrived):
            events.pop(0)()
        index = expert_index(z + dz, x + dx, 1 - core)
        for all_ref, order in arrays:
            j, i = (offset_slot(dz), offset_slot(dx)) if order == 0 else (offset_slot(dx), offset_slot(dz))
            arrive(order, 20 + 4 * j + i, block(all_ref, index))
        chip = index // 2
        for all_ref, target, weighted in ((tok_all, xg, False), (grad_all, sg, True)):
            pick = pick_rows(meta_all, chip, weighted)
            if not weighted:
                flat = jnp.concatenate([pick, jnp.zeros((32, 256), jnp.float32)], axis=0)
                flipped_picks[unit] = flat.T.astype(jnp.bfloat16)
            pick = pick.astype(jnp.bfloat16)

            def columns(n, _, pick=pick, all_ref=all_ref, target=target):
                cols = pl.ds(pl.multiple_of(n * WIDE_D, WIDE_D), WIDE_D)
                rows = dot(pick, all_ref[chip, :, cols]).astype(jnp.bfloat16)
                for e in range(2):
                    target[e, 48 * k:48 * k + 48, cols] = rows[48 * e:48 * e + 48]
                return 0

            lax.fori_loop(0, 2048 // WIDE_D, columns, 0)

    def forward(first, count):
        place = slice(first, first + count)

        def one(e, _):
            rows = xg[e, 0:count]
            gate_linear = dot(rows, gate[e])
            up_linear = dot(rows, up[e])
            delta_hidden = dot(sg[e, 0:count], down[e], NT)
            logistic = jax.nn.sigmoid(gate_linear)
            activated = gate_linear * logistic
            hid[e, place] = (activated * up_linear).astype(jnp.bfloat16)
            delta_gate = (delta_hidden * up_linear * logistic * (1.0 + gate_linear * (1.0 - logistic))).astype(jnp.bfloat16)
            delta_up = (delta_hidden * activated).astype(jnp.bfloat16)
            deltas[e, place, 0:384] = delta_gate
            deltas[e, place, 384:768] = delta_up

            def columns(n, _):
                at_n = pl.ds(pl.multiple_of(n * WIDE_F, WIDE_F), WIDE_F)
                pg[e, 0:count, at_n] = dot(delta_gate, gate[e, at_n, :], NT) + dot(delta_up, up[e, at_n, :], NT)
                return 0

            lax.fori_loop(0, 2048 // WIDE_F, columns, 0)
            return 0

        return one

    dense = []

    def combine(k, dz, dx, span):
        chip = expert_index(z + dz, x + dx, 0) // 2
        n_dense = len(dense)
        if n_dense >= STAGES:
            for copy in dense[n_dense - STAGES]:
                copy()
        here = n_dense % STAGES
        empty = jnp.zeros((32, span), jnp.float32)

        def columns(n, _):
            cols = pl.ds(pl.multiple_of(n * span, span), span)
            rows = jnp.concatenate([pg[0, 48 * k:48 * k + 48, cols], pg[1, 48 * k:48 * k + 48, cols], empty], axis=0)
            stage[here, :, cols] = dot(flipped_picks[n_dense], rows.astype(jnp.bfloat16)).astype(jnp.bfloat16)
            return 0

        lax.fori_loop(0, 2048 // span, columns, 0)
        kept = pltpu.make_async_copy(
            stage.at[here, pl.ds(pl.multiple_of(core * 128, 128), 128)], mine_hbm.at[chip], dense_local.at[n_dense])
        given = remote(
            stage.at[here, pl.ds(pl.multiple_of((1 - core) * 128, 128), 128)], theirs_hbm.at[chip],
            dense_send.at[n_dense], dense_recv.at[n_dense], expert=pair)
        kept.start()
        given.start()
        dense.append((kept.wait, given.wait_send))

    tables_here = []

    def tables():
        def got_table(i, _):
            peer = (me + N_EXPERT - i) % N_EXPERT
            remote(meta_send.at[peer], meta_all.at[peer], msend.at[i], mrecv.at[i], expert=peer).wait_recv()
            return 0

        lax.fori_loop(1, N_EXPERT, got_table, 0)

    stores, kept_deltas = [], []
    run_events(4)
    tables()
    first = 0
    for g, chips in enumerate(GROUPS):
        count = 48 * len(chips)
        after_dispatch, after_one, after_two, after_combine = PLAN[g]
        for copy in stores:
            copy.wait()
        for k, (dz, dx) in enumerate(chips):
            dispatch(first // 48 + k, k, dz, dx)
            run_events(after_dispatch)
        stores = [
            pltpu.make_async_copy(xg.at[:, pl.ds(0, count)], x_hbm.at[:, pl.ds(first, count)], local_sems.at[5]),
            pltpu.make_async_copy(sg.at[:, pl.ds(0, count)], s_hbm.at[:, pl.ds(first, count)], local_sems.at[6]),
        ]
        for copy in stores:
            copy.start()
        if g == 0:
            for copy in weights:
                copy.wait()
        one = forward(first, count)
        if g < 3:
            one(0, 0)
            run_events(after_one)
            one(1, 0)
            run_events(after_two)
        else:
            lax.fori_loop(0, 2, one, 0)
        keep = pltpu.make_async_copy(
            deltas.at[:, pl.ds(first, count)], gu_hbm.at[:, pl.ds(first, count)], local_sems.at[7 + g])
        keep.start()
        kept_deltas.append(keep)
        for k, (dz, dx) in enumerate(chips):
            combine(k, dz, dx, WIDE_C if g < 3 else 2048)
            run_events(after_combine)
        first += count
        if g >= 2:
            begin, end = ((0, 512), (512, 768))[g - 2]
            for e in range(2):
                h_out[e, :, begin:end] = hid[e, begin:end].astype(jnp.float32).T.astype(jnp.bfloat16)
    assert not events
    total = jnp.zeros((8, 128), jnp.float32)
    for s in range(N_EXPERT):
        total = total + meta_all[s]
    plane_out[...] = total

    def sent_table(i, _):
        peer = (me + i) % N_EXPERT
        remote(meta_send.at[peer], meta_all.at[me], msend.at[i], mrecv.at[i], expert=peer).wait_send()
        return 0

    lax.fori_loop(1, N_EXPERT, sent_table, 0)
    for copy in stores + kept_deltas:
        copy.wait()
    for copy in started:
        copy.wait_send()
    for waits in dense[-STAGES:]:
        for wait in waits:
            wait()
    n_dense = 0
    for chips in GROUPS:
        for dz, dx in chips:
            chip = expert_index(z + dz, x + dx, 0) // 2
            remote(
                theirs_hbm.at[chip], theirs_hbm.at[chip], dense_send.at[n_dense], dense_recv.at[n_dense], expert=pair
            ).wait_recv()
            n_dense += 1


VMEM_LIMIT = 67_000_000
LOAD_SCALE = 2 * N_EXPERT / (N_EXPERT * N_DP * 128 * 8)


def forward_pass(ids, routes, tokens, grads, gate, up, down):
    vmem = pl.BlockSpec(memory_space=pltpu.VMEM)
    anywhere = pl.BlockSpec(memory_space=pl.ANY)
    rows, width = tokens.shape
    hidden = gate.shape[2]
    chips = N_EXPERT // 2
    slots = chips * 2 * CAP
    bf16 = jnp.bfloat16
    dma = pltpu.SemaphoreType.DMA
    return pl.pallas_call(
        forward_kernel,
        out_shape=(
            jax.ShapeDtypeStruct((2, slots, width), bf16),
            jax.ShapeDtypeStruct((2, slots, width), bf16),
            jax.ShapeDtypeStruct((2, slots, 2 * hidden), bf16),
            jax.ShapeDtypeStruct((2, hidden, slots), bf16),
            jax.ShapeDtypeStruct((chips, rows, width), bf16),
            jax.ShapeDtypeStruct((chips, rows, width), bf16),
            jax.ShapeDtypeStruct((8, 128), jnp.float32),
        ),
        in_specs=[vmem] * 2 + [anywhere] * 5,
        out_specs=(anywhere, anywhere, anywhere, vmem, anywhere, anywhere, vmem),
        scratch_shapes=[
            pltpu.VMEM((chips, 2 * rows, width), bf16),
            pltpu.VMEM((chips, 2 * rows, width), bf16),
            pltpu.VMEM((N_EXPERT, 8, 128), jnp.float32),
            pltpu.VMEM((N_EXPERT, 8, 128), jnp.float32),
            pltpu.VMEM(gate.shape, bf16),
            pltpu.VMEM(up.shape, bf16),
            pltpu.VMEM(down.shape, bf16),
            pltpu.VMEM((2, MOST, width), bf16),
            pltpu.VMEM((2, MOST, width), bf16),
            pltpu.VMEM((2, slots, 2 * hidden), bf16),
            pltpu.VMEM((2, slots, hidden), bf16),
            pltpu.VMEM((2, MOST, width), jnp.float32),
            pltpu.VMEM((STAGES, 2 * rows, width), bf16),
            pltpu.VMEM((chips, 2 * rows, 128), bf16),
            dma((N_EXPERT,)), dma((N_EXPERT,)),
            dma((2, 36)), dma((2, 36)),
            dma((chips,)), dma((chips,)), dma((chips,)),
            dma((11,)),
        ],
        compiler_params=pltpu.CompilerParams(collective_id=0, has_side_effects=True, vmem_limit_bytes=VMEM_LIMIT),
        name="forward_pass",
    )(ids, routes, tokens, grads, gate, up, down)


def finish_kernel(
    x_hbm, s_hbm, gu_hbm, h_hbm, mine_hbm, theirs_hbm, sums_ref,
    gi_out, gate_out, up_out, d_out, load_out,
    xv, sv, deltas, hid, sums_out, blk, theirs, tx_gu, tx_d, far_gu, far_d, rx_gu, rx_d, q_far, q_near, p_far, p_near,
    far_send, far_recv, near_send, near_recv, qf_send, qf_recv, qn_send, qn_recv,
    pf_send, pf_recv, pn_send, pn_recv, ssend, srecv, local_sems,
):
    me = lax.axis_index("expert")
    y = lax.axis_index("dp")
    z, x, core = me // (2 * SIDE), (me // 2) % SIDE, me % 2
    peers = ((y + 1) % N_DP, (y + 3) % N_DP)
    far_y = (y + 2) % N_DP

    barrier = pltpu.get_barrier_semaphore()
    neighbours = [
        expert_index(z + 1, x, core), expert_index(z - 1, x, core),
        expert_index(z, x + 1, core), expert_index(z, x - 1, core),
    ]
    for peer in neighbours:
        pl.semaphore_signal(barrier, inc=1, device_id={"expert": peer}, device_id_type=MESH)
    for peer in (*peers, far_y):
        pl.semaphore_signal(barrier, inc=1, device_id={"dp": peer}, device_id_type=MESH)
    loads = []
    for n, (hbm, vmem) in enumerate((
        (x_hbm.at[0], xv.at[0]), (gu_hbm.at[0], deltas.at[0]), (x_hbm.at[1], xv.at[1]), (gu_hbm.at[1], deltas.at[1]),
        (s_hbm, sv), (h_hbm, hid), (mine_hbm, blk), (theirs_hbm, theirs),
    )):
        load = pltpu.make_async_copy(hbm, vmem, local_sems.at[n])
        load.start()
        loads.append(load)

    started = []

    def send(copy):
        copy.start()
        started.append(copy)

    def weight_slice(slot, e, owner):
        base = pl.multiple_of(owner * 512, 512)

        def columns(n, _):
            cols = pl.ds(pl.multiple_of(base + n * 256, 256), 256)
            rows = pl.ds(pl.multiple_of(n * 256, 256), 256)
            tx_gu[slot, e, rows] = dot(xv[e, :, cols], deltas[e], TN).astype(jnp.bfloat16)
            return 0

        lax.fori_loop(0, 2, columns, 0)

    def down_slice(slot, e, owner):
        rows = hid[e, pl.ds(pl.multiple_of(owner * 96, 96), 96), :]

        def columns(n, _):
            cols = pl.ds(pl.multiple_of(n * 1024, 1024), 1024)
            tx_d[slot, e, :, cols] = dot(rows, sv[e, :, cols]).astype(jnp.bfloat16)
            return 0

        lax.fori_loop(0, 2, columns, 0)

    def by_rows(first, count, body):
        def step(i, _):
            body(pl.ds(pl.multiple_of(first + i * 32, 32), 32))
            return 0

        lax.fori_loop(0, count // 32, step, 0)

    def wide(value):
        return value.astype(jnp.float32)

    kinds = ((weight_slice, tx_gu, far_gu, rx_gu), (down_slice, tx_d, far_d, rx_d))

    def at(order, dp_, dq):
        return (expert_index(z + dp_, x + dq, core) if order == 0 else expert_index(z + dq, x + dp_, core)) // 2

    def device(order, dp_, dq):
        return expert_index(z + dp_, x + dq, core) if order == 0 else expert_index(z + dq, x + dp_, core)

    def cols_of(h):
        return pl.ds(1024 * h, 1024)

    top, bottom = pl.ds(0, 64), pl.ds(64, 64)
    parts = (top, bottom)
    whole = pl.ds(0, 128)
    steps = (1, -1)

    for kind, (compute, tx, far, rx) in enumerate(kinds):
        for side in (0, 1):
            for load in loads[2 * side:2 * side + 2] if kind == 0 else loads[4:6] if side == 0 else ():
                load.wait()
            compute(0, side, far_y)
            if kind == 0 and side == 0:
                pl.semaphore_wait(barrier, 7)
            send(remote(tx.at[0, side], far.at[side], far_send.at[side, kind], far_recv.at[side, kind], dp=peers[side]))
    for n, other in enumerate((*peers, far_y)):
        send(remote(sums_ref, sums_out.at[n], ssend.at[n], srecv.at[n], dp=other))

    loads[6].wait()
    loads[7].wait()

    def add_partner(i, _):
        chip = i // 4
        rows = pl.ds(pl.multiple_of(i % 4 * 32, 32), 32)
        blk[chip, rows] = (wide(blk[chip, rows]) + wide(theirs[chip, rows])).astype(jnp.bfloat16)
        return 0

    lax.fori_loop(0, N_EXPERT * 2, add_partner, 0)
    for j in range(4):
        for h in range(2):
            for side in (0, 1):
                send(remote(
                    blk.at[at(h, OFFSETS[j], 2), parts[side], cols_of(h)], q_far.at[h, j, parts[side]],
                    qf_send.at[h, j, side], qf_recv.at[h, j, side], expert=device(h, 0, steps[side]),
                ))

    for kind, (compute, tx, far, rx) in enumerate(kinds):
        for side in (0, 1):
            compute(1 + side, 1 - side, peers[side])
            send(remote(
                tx.at[1 + side, 1 - side], rx.at[side, 1 - side],
                near_send.at[side, 1 - side, kind], near_recv.at[side, 1 - side, kind], dp=peers[side],
            ))

    for j in (3, 1, 2, 0):
        for h in range(2):
            for side in (0, 1):
                piece = q_far.at[h, j, parts[side]]
                remote(piece, piece, qf_send.at[h, j, side], qf_recv.at[h, j, side], expert=device(h, 0, 1)).wait_recv()
                index = at(h, OFFSETS[j], steps[side])

                def add_far(rows, index=index, h=h, j=j):
                    blk[index, rows, cols_of(h)] = (
                        wide(blk[index, rows, cols_of(h)]) + wide(q_far[h, j, rows])).astype(jnp.bfloat16)

                by_rows(64 * side, 64, add_far)
                send(remote(
                    blk.at[index, whole, cols_of(h)], q_near.at[h, j, side],
                    qn_send.at[h, j, side], qn_recv.at[h, j, side], expert=device(h, 0, steps[side]),
                ))

    for kind, (compute, tx, far, rx) in enumerate(kinds):
        for side in (0, 1):
            compute(1 + side, side, peers[side])
            piece = far.at[side]
            remote(piece, piece, far_send.at[side, kind], far_recv.at[side, kind], dp=peers[0]).wait_recv()

            def add_far(rows, tx=tx, far=far, side=side):
                tx[1 + side, side, rows] = (wide(tx[1 + side, side, rows]) + wide(far[side, rows])).astype(jnp.bfloat16)

            by_rows(0, tx.shape[2], add_far)
            send(remote(
                tx.at[1 + side, side], rx.at[side, side],
                near_send.at[side, side, kind], near_recv.at[side, side, kind], dp=peers[side],
            ))

    def second_axis_sum(h, j):
        index = at(h, OFFSETS[j], 0)
        for side in (0, 1):
            piece = q_near.at[h, j, side]
            remote(piece, piece, qn_send.at[h, j, side], qn_recv.at[h, j, side], expert=device(h, 0, 1)).wait_recv()

        def add_near(rows):
            blk[index, rows, cols_of(h)] = (
                wide(blk[index, rows, cols_of(h)]) + wide(q_near[h, j, 0, rows]) + wide(q_near[h, j, 1, rows])
            ).astype(jnp.bfloat16)

        by_rows(0, 128, add_near)
        return index

    for h in range(2):
        index = second_axis_sum(h, 3)
        for side in (0, 1):
            send(remote(
                blk.at[index, parts[side], cols_of(h)], p_far.at[h, parts[side]],
                pf_send.at[h, side], pf_recv.at[h, side], expert=device(h, steps[side], 0),
            ))
    for side in (0, 1):
        for h in range(2):
            index = second_axis_sum(h, 2 if side == 0 else 1)
            piece = p_far.at[h, parts[side]]
            remote(piece, piece, pf_send.at[h, side], pf_recv.at[h, side], expert=device(h, 1, 0)).wait_recv()

            def add_far(rows, index=index, h=h):
                blk[index, rows, cols_of(h)] = (
                    wide(blk[index, rows, cols_of(h)]) + wide(p_far[h, rows])).astype(jnp.bfloat16)

            by_rows(64 * side, 64, add_far)
            send(remote(
                blk.at[index, whole, cols_of(h)], p_near.at[h, side],
                pn_send.at[h, side], pn_recv.at[h, side], expert=device(h, steps[side], 0),
            ))
    for kind, (compute, tx, far, rx) in enumerate(kinds):
        for e in (0, 1):
            compute(3, e, y)
    for h in range(2):
        index = second_axis_sum(h, 0)
        for side in (0, 1):
            piece = p_near.at[h, side]
            remote(piece, piece, pn_send.at[h, side], pn_recv.at[h, side], expert=device(h, 1, 0)).wait_recv()

        def add_last(rows, index=index, h=h):
            gi_out[rows, cols_of(h)] = (
                wide(blk[index, rows, cols_of(h)]) + wide(p_near[h, 0, rows]) + wide(p_near[h, 1, rows])
            ).astype(jnp.bfloat16)

        by_rows(0, 128, add_last)
    for n in range(3):
        remote(sums_ref, sums_out.at[n], ssend.at[n], srecv.at[n], dp=far_y).wait_recv()
    load_out[...] = (sums_ref[...] + sums_out[0] + sums_out[1] + sums_out[2]) * LOAD_SCALE
    factor = 1.0 / N_DP
    for kind, (compute, tx, far, rx) in enumerate(kinds):
        for e in (0, 1):
            for side in (0, 1):
                piece = rx.at[side, e]
                remote(piece, piece, near_send.at[side, e, kind], near_recv.at[side, e, kind], dp=far_y).wait_recv()

            def total(rows, kind=kind, e=e, tx=tx, rx=rx):
                value = ((wide(tx[3, e, rows]) + wide(rx[0, e, rows]) + wide(rx[1, e, rows])) * factor).astype(jnp.bfloat16)
                if kind == 0:
                    gate_out[e, rows] = value[:, 0:384]
                    up_out[e, rows] = value[:, 384:768]
                else:
                    d_out[e, rows] = value

            by_rows(0, tx.shape[2], total)
    for copy in started:
        copy.wait_send()


def finish(xs, ss, gu, h, mine, theirs, sums):
    vmem = pl.BlockSpec(memory_space=pltpu.VMEM)
    anywhere = pl.BlockSpec(memory_space=pl.ANY)
    bf16 = jnp.bfloat16
    chips, rows, width = mine.shape
    hidden, slots = h.shape[1:]
    tile = (8, 128)
    wide, deep = (width // N_DP, 2 * hidden), (hidden // N_DP, width)
    near = (2, width // N_DP, hidden)
    dma = pltpu.SemaphoreType.DMA
    buf = lambda *shape: pltpu.VMEM(shape, bf16)
    return pl.pallas_call(
        finish_kernel,
        out_shape=(
            jax.ShapeDtypeStruct((rows, width), bf16),
            jax.ShapeDtypeStruct(near, bf16),
            jax.ShapeDtypeStruct(near, bf16),
            jax.ShapeDtypeStruct((2, *deep), bf16),
            jax.ShapeDtypeStruct(tile, jnp.float32),
        ),
        in_specs=[anywhere] * 6 + [vmem],
        out_specs=(vmem,) * 5,
        scratch_shapes=[
            buf(2, slots, width), buf(2, slots, width), buf(2, slots, 2 * hidden), buf(2, hidden, slots),
            pltpu.VMEM((3, *tile), jnp.float32), buf(chips, rows, width), buf(chips, rows, width),
            buf(4, 2, *wide), buf(4, 2, *deep), buf(2, *wide), buf(2, *deep), buf(2, 2, *wide), buf(2, 2, *deep),
            buf(2, 4, rows, width // 2), buf(2, 4, 2, rows, width // 2),
            buf(2, rows, width // 2), buf(2, 2, rows, width // 2),
            dma((2, 2)), dma((2, 2)), dma((2, 2, 2)), dma((2, 2, 2)),
            dma((2, 4, 2)), dma((2, 4, 2)), dma((2, 4, 2)), dma((2, 4, 2)),
            dma((2, 2)), dma((2, 2)), dma((2, 2)), dma((2, 2)),
            dma((3,)), dma((3,)), dma((8,)),
        ],
        compiler_params=pltpu.CompilerParams(collective_id=1, has_side_effects=True, vmem_limit_bytes=VMEM_LIMIT),
        name="finish",
    )(xs, ss, gu, h, mine, theirs, sums)


def shards(tokens, out_grad, route_weights, expert_ids, gate_weight, up_weight, down_weight):
    rows, width = tokens.shape
    num_experts = 2 * N_EXPERT
    routes = route_weights.astype(jnp.float32)
    xs, ss, gu, h, mine, theirs, plane = forward_pass(
        expert_ids.T, routes.T, tokens, out_grad, gate_weight, up_weight, down_weight
    )
    grad_input, grad_gate, grad_up, grad_down, load = finish(xs, ss, gu, h, mine, theirs, plane)
    return grad_input, grad_gate, grad_up, grad_down, load[4, :num_experts]


def solution(mesh):
    return jax.shard_map(
        shards,
        mesh=mesh,
        in_specs=(
            P(("expert", "dp"), None),
            P(("expert", "dp"), None),
            P(("expert", "dp"), None),
            P(("expert", "dp"), None),
            P("expert", None, None),
            P("expert", None, None),
            P("expert", None, None),
        ),
        out_specs=(
            P(("expert", "dp"), None),
            P("expert", "dp", None),
            P("expert", "dp", None),
            P("expert", "dp", None),
            P(),
        ),
        check_vma=False,
    )
```
